256 devices in a mesh: region: 32 (over x, z), order: 8 (over y, core).
Axes of the slice: x: 4, y: 4, z: 8, core: 2. Of those that a mesh axis runs over, the one named last changes fastest.
Arguments:
- runoff: float32 [240, 32, 8192], P(None, None, ('region', 'order')), may hold values from 0.01 to 2
- send_rows: int32 [32, 8, 128], P('region', 'order'), may hold values from 0 to 31
- remap_index: int32 [32768, 4], P(('region', 'order')), may hold values from 0 to 127
- remap_weight: float32 [32768, 4], P(('region', 'order')), may hold values from 0.05 to 1
- class_id: int32 [32768, 1], P(('region', 'order')), may hold values from 0 to 7; in each aligned block of 128 rows (0 to 127, 128 to 255, ...) at most 32 rows name the same one
- kernel_shape: float32 [8, 240], replicated, may hold values from 0.5 to 2
- kernel_rate: float32 [8], replicated, may hold values from 0.01 to 0.3
- outlets: int32 [32, 8, 32], P('region', 'order'), may hold values from 0 to 127, as said below
- incidence: int32 [32, 8, 32, 128], P('region', 'order'), may hold values from 0 to 1, as said below
Outputs:
- outflow: bfloat16 [240, 32, 32768], P(None, None, ('region', 'order'))
The draws below stay inside these ranges and needn't reach their ends.
Inputs may be any that keep to these rules, and one draw needn't show every extreme that they name: `send_rows`: row of the sending device's own grid rows. `class_id`: no class is named by more than 32 reaches of one device; on some device a class has exactly 32. `outlets`: the 32 outlet numbers of one device are distinct. `incidence`: each row has exactly one 1; no column of one device has more than one 1.
All inputs are finite; a program needn't handle non-finite values.
Results may differ from the reference program's by a relative error of at most 0.0038.
Values may be sent and summed in bfloat16 or wider, within the bound.
A program may use at most 128 MiB of HBM per device.

```python
import math
import jax
import jax.numpy as jnp
import numpy as np
from jax import lax

H = 240
M = 32
K = 4
NCLASS = 8
OUT = 32
SLOT = 4
GRID_DEV = 32
CAT = 128
CAP = 32
RECV = 128
GRID = 8192
CATS = 32768
N_REGION = 32
N_ORDER = 8


def network(key):
    base_key = jax.random.fold_in(key, 11)
    first_key, second_key, third_key = jax.random.split(base_key, 3)
    device_count = N_REGION * N_ORDER
    through = OUT - OUT // 8
    orders = jax.vmap(lambda one_key: jax.random.permutation(one_key, CAT))(jax.random.split(first_key, device_count))
    outlet_ids = orders[:, :OUT]
    picks = jax.vmap(lambda one_key: jax.random.permutation(one_key, OUT))(jax.random.split(second_key, device_count))
    chosen = jnp.take_along_axis(outlet_ids, picks[:, :through], axis=1)
    others = orders[:, OUT:2 * OUT - through]
    targets = jnp.concatenate([chosen, others], axis=1)
    mixing = jax.vmap(lambda one_key: jax.random.permutation(one_key, OUT))(jax.random.split(third_key, device_count))
    targets = jnp.take_along_axis(targets, mixing, axis=1)
    return (outlet_ids.reshape(N_REGION, N_ORDER, OUT), targets.reshape(N_REGION, N_ORDER, OUT))


def draw_outlets(key, part):
    return network(key)[0].astype(jnp.int32)


def draw_incidence(key, part):
    targets = network(key)[1]
    return (targets[..., None] == jnp.arange(CAT)[None, None, None, :]).astype(jnp.int32)


def place_ends(entries, own_key, smallest, largest):
    longest = entries.shape.index(max(entries.shape))
    spots = []
    for shift in (0, 1):
        where = [jax.random.randint(jax.random.fold_in(own_key, axis), (), 0, length) for axis, length in enumerate(entries.shape)]
        where[longest] = (where[longest] + shift) % entries.shape[longest]
        spots.append(tuple(where))
    return entries.at[spots[0]].set(smallest).at[spots[1]].set(largest)


def shard_levels(rng, shape, pieces, low, largest):
    level = 1.0
    for position, shards_of in pieces:
        steps = jax.random.uniform(jax.random.fold_in(jax.random.fold_in(rng, 6), position), (shards_of,), jnp.float32, low / len(pieces), largest / len(pieces))
        level = level * jnp.repeat(jnp.exp(steps), shape[position] // shards_of).reshape((-1,) + (1,) * (len(shape) - 1 - position))
    return level


def assign_block(own_key, own, number, rows, number_of, top, limit, lean):
    sequence = jax.random.permutation(own_key, number_of)
    packed, usual = portions_of(number_of, rows * top, limit, lean, True), portions_of(number_of, rows * top, limit, lean, False)
    places = jnp.arange(number_of)

    def named(tallies, turn):
        used = int((tallies > 0).sum())
        fixed = max(1, used // 4)
        shifted = fixed + (places - fixed + turn * (used - fixed)) % max(1, number_of - fixed)
        return jnp.zeros((number_of,), jnp.int32).at[sequence[jnp.where(places < fixed, places, shifted)]].set(jnp.asarray(tallies, jnp.int32))

    tallies = jnp.where(number % 4 == 0, named(packed, number // 4), named(usual, number - number // 4 - 1))
    mixed = jax.random.permutation(jax.random.fold_in(own, 3), number_of)
    donor, taker = mixed[0:number_of // 2 * 2:2], mixed[1:number_of // 2 * 2:2]
    slack = jnp.minimum(tallies[donor] - 1, limit - tallies[taker]) // 2
    slack = jnp.where((donor == sequence[0]) | (taker == sequence[0]) | (tallies[taker] == 0), 0, jnp.maximum(slack, 0))
    shifted = jax.random.randint(jax.random.fold_in(own, 4), (number_of // 2,), 0, 1 << 20) % (slack + 1)
    tallies = tallies.at[donor].add(-shifted).at[taker].add(shifted)
    labels = jnp.searchsorted(jnp.cumsum(tallies), jnp.arange(rows * top), side="right").astype(jnp.int32)
    grid = labels.reshape(top, rows).T
    grid = grid[jax.random.permutation(jax.random.fold_in(own, 1), rows)]
    turn = jax.random.randint(jax.random.fold_in(own, 2), (rows, 1), 0, top)
    return jnp.take_along_axis(grid, (jnp.arange(top)[None, :] + turn) % top, axis=1)


def portions_of(number_of, total, reach, slope, full):
    loads = [(1 << 20) // math.isqrt(rank ** slope) + 1 for rank in range(1, number_of + 1)]
    largest = reach if full else min(reach, max(-(-total // number_of), total * loads[0] // sum(loads)))
    least = 1 if total - largest >= number_of - 1 else 0
    holding, surplus = [largest] + [least] * (number_of - 1), total - largest - least * (number_of - 1)
    while surplus > 0:
        movable = [i for i in range(1, number_of) if holding[i] < largest] or [i for i in range(1, number_of) if holding[i] < reach]
        mass, left = sum([loads[i] for i in movable]), surplus
        for i in movable:
            extra = min(reach - holding[i], max(1, left * loads[i] // mass), surplus)
            holding[i] = holding[i] + extra
            surplus = surplus - extra
    return np.array(holding)


def setup_inputs(seed: int = 0) -> dict:
    keys = jax.random.split(jax.random.key(seed), 10)
    runoff = jnp.clip(jnp.exp(math.log(2.0) - 5.2983174 * jax.random.uniform(keys[0], (H, M, GRID), jnp.float32) ** shard_levels(keys[0], (H, M, GRID), ((2, 256),), -0.2, 0.2)), 0.01, 2.0)
    send_rows = place_ends(jax.random.randint(keys[1], (N_REGION, N_ORDER, RECV), 0, GRID_DEV), jax.random.fold_in(keys[1], 1), 0, GRID_DEV - 1).astype(jnp.int32)
    remap_index = place_ends(jax.random.randint(keys[2], (CATS, K), 0, RECV), jax.random.fold_in(keys[2], 1), 0, RECV - 1).astype(jnp.int32)
    remap_weight = jnp.clip(jnp.exp(math.log(1.0) - 2.9957323 * jax.random.uniform(keys[3], (CATS, K), jnp.float32) ** shard_levels(keys[3], (CATS, K), ((0, 256),), -0.2, 0.2)), 0.05, 1.0)
    class_id_keys = jax.random.split(jax.random.fold_in(keys[4], 1), CATS // CAT)
    class_id_turns = jax.random.permutation(jax.random.fold_in(keys[4], 3), CATS // CAT)
    class_id = jax.vmap(lambda own, number: assign_block(jax.random.fold_in(keys[4], 2), own, number, CAT, NCLASS, 1, CAP, 2))(class_id_keys, class_id_turns).reshape((CATS, 1))
    kernel_shape = jnp.clip(jnp.exp(jax.random.uniform(keys[5], (NCLASS, H), jnp.float32, math.log(0.5), math.log(2.0))), 0.5, 2.0)
    kernel_rate = jnp.clip(jnp.exp(jax.random.uniform(keys[6], (NCLASS,), jnp.float32, math.log(0.01), math.log(0.3))), 0.01, 0.3)
    outlets = draw_outlets(jax.random.fold_in(keys[9], 71), 0)
    incidence = draw_incidence(jax.random.fold_in(keys[9], 71), 0)
    return {"runoff": runoff, "send_rows": send_rows, "remap_index": remap_index, "remap_weight": remap_weight, "class_id": class_id, "kernel_shape": kernel_shape, "kernel_rate": kernel_rate, "outlets": outlets, "incidence": incidence}


def kernels(kernel_shape, kernel_rate):
    lag_hours = jnp.arange(H, dtype=jnp.float32)
    kernel = kernel_rate[:, None] * kernel_shape * jnp.exp(-kernel_rate[:, None] * lag_hours[None, :])
    rounded = lax.optimization_barrier(kernel.astype(jnp.bfloat16))
    return rounded.astype(jnp.float32)


def convolve(signal, kernel_rows):
    length = 2 * H
    signal_freq = jnp.fft.rfft(signal, n=length, axis=0)
    kernel_freq = jnp.fft.rfft(kernel_rows.T, n=length, axis=0)
    return jnp.fft.irfft(signal_freq * kernel_freq[:, None, :], n=length, axis=0)[:H]


def reference(runoff, send_rows, remap_index, remap_weight, class_id, kernel_shape, kernel_rate, outlets, incidence):
    kernel_table = kernels(kernel_shape, kernel_rate)
    grid_rows = runoff.reshape(H, M, N_REGION, N_ORDER, GRID_DEV)
    index_all = remap_index.reshape(N_REGION, N_ORDER, CAT, K)
    weight_all = remap_weight.reshape(N_REGION, N_ORDER, CAT, K)
    class_all = class_id.reshape(N_REGION, N_ORDER, CAT)
    source_region = jnp.arange(N_REGION, dtype=jnp.int32)[:, None, None]
    source_level = jnp.arange(N_ORDER, dtype=jnp.int32)[None, :, None]
    reach_ids = jnp.arange(CAT, dtype=jnp.int32)

    def one_level(panel, inputs):
        received, index, weight, classes, outlet_ids, links = inputs
        lateral = jnp.zeros((H, M, CAT), jnp.float32)
        for column in range(K):
            lateral = lateral + weight[:, column] * jnp.take(received, index[:, column], axis=2)
        lateral = lax.optimization_barrier(lateral.astype(jnp.bfloat16)).astype(jnp.float32)
        base_flow = convolve(lateral, kernel_table[classes])
        targets = jnp.sum(links * reach_ids[None, :], axis=1).astype(jnp.int32)
        routed = convolve(panel.astype(jnp.float32), kernel_table[classes[targets]])
        total = base_flow.at[:, :, targets].add(routed)
        return total[:, :, outlet_ids].astype(jnp.bfloat16), total.astype(jnp.bfloat16)

    def one_region(region):
        chosen = lax.dynamic_slice_in_dim(send_rows, region * SLOT, SLOT, 2)
        gathered = grid_rows[:, :, source_region, source_level, chosen]
        gathered = jnp.transpose(gathered, (3, 0, 1, 2, 4)).reshape(N_ORDER, H, M, RECV)
        start = jnp.zeros((H, M, OUT), jnp.bfloat16)
        inputs = (gathered, index_all[region], weight_all[region], class_all[region], outlets[region], incidence[region])
        unused, flows = lax.scan(one_level, start, inputs)
        return flows

    every = lax.map(one_region, jnp.arange(N_REGION, dtype=jnp.int32))
    return jnp.transpose(every, (2, 3, 0, 1, 4)).reshape(H, M, N_REGION * N_ORDER * CAT)
```

```python
import functools

import jax
import jax.numpy as jnp
from jax import lax
from jax.experimental import pallas as pl
from jax.experimental.pallas import tpu as pltpu
from jax.sharding import PartitionSpec as P

MESH = pl.DeviceIdType.MESH
BF = jnp.bfloat16
F32 = jnp.float32
LANES = 256
MG = 4


def mm(a, b):
    return jnp.dot(a, b, preferred_element_type=F32)


def mm_nt(a, b):
    return lax.dot_general(a, b, (((1,), (1,)), ((), ())), preferred_element_type=F32)


def iota(shape, dim):
    return lax.broadcasted_iota(jnp.int32, shape, dim)


def onehot(hits):
    return jnp.where(hits, 1.0, 0.0)


def kernel(
    sizes,
    x_ref,
    send_rows_ref,
    idx_ref,
    w_ref,
    cls_ref,
    shape_ref,
    rate_ref,
    outlets_ref,
    inc_ref,
    out_ref,
    xb,
    send,
    recv,
    inbox,
    outbox,
    lat,
    base_out,
    out32,
    sel,
    w_hi,
    w_lo,
    out_sel,
    perm,
    scat,
    mask_o,
    mask_c,
    toep,
    toep_t,
    ssem,
    rsem,
    cssem,
    crsem,
):
    hours, members, regions, orders, reaches, classes, panel = sizes
    groups = members // MG
    slots = send.shape[2] * regions
    r = lax.axis_index("region")
    o = lax.axis_index("order")
    nxt = lax.rem(o + 1, orders)
    prv = lax.rem(o + orders - 1, orders)

    barrier = pltpu.get_barrier_semaphore()

    def greet(d, c):
        peer = lax.rem(r + d, regions)
        pl.semaphore_signal(barrier, inc=1, device_id=(peer, o), device_id_type=MESH)
        return c

    lax.fori_loop(1, regions, greet, 0)
    pl.semaphore_signal(barrier, inc=1, device_id=(r, nxt), device_id_type=MESH)
    pl.semaphore_signal(barrier, inc=1, device_id=(r, prv), device_id_type=MESH)

    n0 = iota((slots, 128), 0)
    c1 = iota((slots, 128), 1)
    spread = onehot(c1 == (n0 >> 4) * 4 + (n0 & 3)).astype(BF)
    row_hit = onehot(send_rows_ref[...] == (iota((128, 128), 0) & 31)).astype(BF)
    picked = mm_nt(spread, row_hit)
    sel[...] = jnp.where(((n0 >> 2) & 3) == (c1 >> 5), picked, 0.0).astype(BF)
    xb[:, 128:LANES] = jnp.zeros((xb.shape[0], LANES - 128), BF)

    pl.semaphore_wait(barrier, regions + 1)

    def dispatch(g, c):
        rows = MG * 32
        start = pl.multiple_of(g * rows, rows)
        xb[:, 0:hours] = x_ref[pl.ds(start, rows), :].astype(BF)
        send[g] = mm(sel[...], xb[...]).astype(BF).reshape(send.shape[1:])
        pltpu.make_async_copy(send.at[g, r], recv.at[g, r], rsem.at[g]).start()

        def push(d, c):
            peer = lax.rem(r + d, regions)
            pltpu.make_async_remote_copy(
                src_ref=send.at[g, peer],
                dst_ref=recv.at[g, r],
                send_sem=ssem.at[g],
                recv_sem=rsem.at[g],
                device_id=(peer, o),
                device_id_type=MESH,
            ).start()
            return c

        return lax.fori_loop(1, regions, push, c)

    lax.fori_loop(0, groups, dispatch, 0)

    diag = iota((classes, classes), 0) == iota((classes, classes), 1)
    rate = jnp.sum(
        jnp.where(diag, jnp.broadcast_to(rate_ref[...], (classes, classes)), 0.0),
        axis=1,
        keepdims=True,
    )
    lag = iota((classes, hours), 1).astype(F32)
    unit = rate * shape_ref[...] * jnp.exp(-rate * lag)
    base_out[0:classes, 128:LANES] = jnp.zeros((classes, LANES - 128), F32)
    base_out[0:classes, 0:hours] = unit.astype(BF).astype(F32)
    later = iota((LANES, LANES), 1) >= iota((LANES, LANES), 0)

    def table(k, c):
        row = jnp.broadcast_to(base_out[pl.ds(k, 1), :], (LANES, LANES))
        turned = pltpu.roll(row, 0, 1, stride=1, stride_axis=0)
        turned = jnp.where(later, turned, 0.0)
        at = pl.multiple_of(k * LANES, LANES)
        toep_t[pl.ds(at, LANES), :] = turned.astype(BF)
        toep[:, pl.ds(at, LANES)] = turned.T.astype(BF)
        return c

    lax.fori_loop(0, classes, table, 0)

    pos = (n0 >> 4) * 4 + (n0 & 3)
    weights_t = jnp.zeros((slots, 128), F32)
    for j in range(4):
        weights_t = weights_t + jnp.where(idx_ref[j : j + 1, :] == pos, w_ref[j : j + 1, :], 0.0)
    weights = weights_t.T
    high = weights.astype(BF)
    low = (weights - high.astype(F32)).astype(BF)
    member_of = (iota((reaches, slots), 1) >> 2) & 3
    for m in range(MG):
        here = onehot(member_of == m).astype(BF)
        w_hi[m * 128 : (m + 1) * 128, :] = high * here
        w_lo[m * 128 : (m + 1) * 128, :] = low * here

    i0 = iota((128, 128), 0)
    i1 = iota((128, 128), 1)
    copies = onehot((iota((128, panel), 0) & 31) == iota((128, panel), 1)).astype(BF)
    at_outlet = onehot(outlets_ref[...] == iota((reaches, panel), 0)).astype(BF)
    outlet_of = mm_nt(copies, at_outlet)
    link_of = mm(copies, inc_ref[...].astype(F32).astype(BF))
    link_t = link_of.T
    for m in range(MG):
        out_sel[:, m * 128 : (m + 1) * 128] = jnp.where((i0 >> 5) == m, outlet_of, 0.0).astype(BF)
        scat[m * 128 : (m + 1) * 128, :] = jnp.where((i1 >> 5) == m, link_t, 0.0).astype(BF)
    outlet_bf = outlet_of.astype(BF)
    joined = mm_nt(outlet_bf, link_of.astype(BF))
    perm[...] = jnp.where((i0 >> 5) == (i1 >> 5), joined, 0.0).astype(BF)
    cls_c = jnp.broadcast_to(cls_ref[...].astype(F32), (128, 128)).T
    cls_o = mm(outlet_bf, cls_c.astype(BF))
    for k in range(classes):
        hit_c = onehot(cls_c == float(k)).astype(BF)
        hit_o = onehot(cls_o == float(k)).astype(BF)
        for a in range(2):
            mask_o[k, :, a * 128 : (a + 1) * 128] = hit_o
            for b in range(2):
                mask_c[k, b * 128 : (b + 1) * 128, a * 128 : (a + 1) * 128] = hit_c

    @pl.when(o == 0)
    def _():
        inbox[...] = jnp.zeros_like(inbox)

    def route(rows):
        total = mm(rows * mask_o[0], toep_t[0:LANES, :])
        for k in range(1, classes):
            total = total + mm(rows * mask_o[k], toep_t[k * LANES : (k + 1) * LANES, :])
        return total

    def group(g, c):
        pltpu.make_async_copy(recv.at[g], recv.at[g], rsem.at[g]).wait()
        got = recv[g].reshape(slots, LANES)
        lat[...] = mm(w_hi[...], got) + mm(w_lo[...], got)
        base = mm(out_sel[...], lat[...].astype(BF)).astype(BF)
        base_out[...] = route(base)

        @pl.when(o == 0)
        def _():
            outbox[g] = base_out[...].astype(BF)

        @pl.when(o > 0)
        def _():
            pltpu.make_async_copy(inbox.at[g], inbox.at[g], crsem.at[g]).wait()
            moved = mm(perm[...], inbox[g]).astype(BF)
            outbox[g] = (base_out[...] + route(moved)).astype(BF)

        @pl.when(o < orders - 1)
        def _():
            pltpu.make_async_remote_copy(
                src_ref=outbox.at[g],
                dst_ref=inbox.at[g],
                send_sem=cssem.at[g],
                recv_sem=crsem.at[g],
                device_id=(r, nxt),
                device_id_type=MESH,
            ).start()

        lat[...] = lat[...] + mm(scat[...], inbox[g])

        def pair(h, c):
            entering = lat[pl.ds(pl.multiple_of(h * 256, 256), 256), :].astype(BF)
            total = mm_nt(toep[:, 0:LANES], entering * mask_c[0])
            for k in range(1, classes):
                at = k * LANES
                total = total + mm_nt(toep[:, at : at + LANES], entering * mask_c[k])
            for m in range(2):
                first = g * MG + h * 2 + m
                out32[pl.ds(first, hours, stride=members), :] = total[
                    0:hours, m * 128 : (m + 1) * 128
                ]
            return c

        return lax.fori_loop(0, 2, pair, c)

    lax.fori_loop(0, groups, group, 0)

    block = hours // 10

    def finish(b, c):
        t = b * block
        rows = block * members
        part = out32[pl.ds(pl.multiple_of(t * members, rows), rows), :]
        out_ref[pl.ds(t, block)] = part.reshape(block, members, 128).astype(BF)
        return c

    lax.fori_loop(0, 10, finish, 0)

    def drain(g, c):
        sent = send.at[g, pl.ds(0, regions - 1)]
        pltpu.make_async_copy(sent, sent, ssem.at[g]).wait()

        @pl.when(o < orders - 1)
        def _():
            pltpu.make_async_copy(outbox.at[g], outbox.at[g], cssem.at[g]).wait()

        return c

    lax.fori_loop(0, groups, drain, 0)


def local(
    regions,
    orders,
    runoff,
    send_rows,
    remap_index,
    remap_weight,
    class_id,
    kernel_shape,
    kernel_rate,
    outlets,
    incidence,
):
    hours, members, rows = runoff.shape
    reaches = remap_index.shape[0]
    classes = kernel_shape.shape[0]
    panel = outlets.shape[2]
    groups = members // MG
    slots = regions * MG * 4
    sizes = (hours, members, regions, orders, reaches, classes, panel)
    vmem = pl.BlockSpec(memory_space=pltpu.VMEM)
    return pl.pallas_call(
        functools.partial(kernel, sizes),
        out_shape=jax.ShapeDtypeStruct((hours, members, reaches), BF),
        in_specs=[vmem] * 9,
        out_specs=vmem,
        scratch_shapes=[
            pltpu.VMEM((MG * rows, LANES), BF),
            pltpu.VMEM((groups, regions, MG * 4, LANES), BF),
            pltpu.VMEM((groups, regions, MG * 4, LANES), BF),
            pltpu.VMEM((groups, MG * panel, LANES), BF),
            pltpu.VMEM((groups, MG * panel, LANES), BF),
            pltpu.VMEM((MG * reaches, LANES), F32),
            pltpu.VMEM((MG * panel, LANES), F32),
            pltpu.VMEM((hours * members, reaches), F32),
            pltpu.VMEM((slots, MG * rows), BF),
            pltpu.VMEM((MG * reaches, slots), BF),
            pltpu.VMEM((MG * reaches, slots), BF),
            pltpu.VMEM((MG * panel, MG * reaches), BF),
            pltpu.VMEM((MG * panel, MG * panel), BF),
            pltpu.VMEM((MG * reaches, MG * panel), BF),
            pltpu.VMEM((classes, MG * panel, LANES), BF),
            pltpu.VMEM((classes, 2 * reaches, LANES), BF),
            pltpu.VMEM((LANES, classes * LANES), BF),
            pltpu.VMEM((classes * LANES, LANES), BF),
            pltpu.SemaphoreType.DMA((groups,)),
            pltpu.SemaphoreType.DMA((groups,)),
            pltpu.SemaphoreType.DMA((groups,)),
            pltpu.SemaphoreType.DMA((groups,)),
        ],
        compiler_params=pltpu.CompilerParams(
            collective_id=0, has_side_effects=True, vmem_limit_bytes=56 << 20
        ),
        name="route_levels",
    )(
        jnp.transpose(runoff, (1, 2, 0)).reshape(members * rows, hours),
        send_rows.reshape(1, -1),
        remap_index.T,
        remap_weight.T,
        class_id.reshape(1, -1),
        kernel_shape,
        kernel_rate.reshape(1, -1),
        outlets.reshape(1, -1),
        incidence.reshape(panel, reaches),
    )


def solution(mesh):
    return jax.shard_map(
        functools.partial(local, mesh.shape["region"], mesh.shape["order"]),
        mesh=mesh,
        in_specs=(
            P(None, None, ("region", "order")),
            P("region", "order", None),
            P(("region", "order"), None),
            P(("region", "order"), None),
            P(("region", "order"), None),
            P(),
            P(),
            P("region", "order", None),
            P("region", "order", None, None),
        ),
        out_specs=P(None, None, ("region", "order")),
        check_vma=False,
    )
```

```python
import functools

import jax
import jax.numpy as jnp
from jax import lax
from jax.experimental import pallas as pl
from jax.experimental.pallas import tpu as pltpu
from jax.sharding import PartitionSpec as P

MESH = pl.DeviceIdType.MESH
BF = jnp.bfloat16
F32 = jnp.float32
LANES = 256
MG = 4


def mm(a, b):
    return jnp.dot(a, b, preferred_element_type=F32)


def mm_nt(a, b):
    return lax.dot_general(a, b, (((1,), (1,)), ((), ())), preferred_element_type=F32)


def iota(shape, dim):
    return lax.broadcasted_iota(jnp.int32, shape, dim)


def onehot(hits):
    return jnp.where(hits, 1.0, 0.0)


def kernel(
    sizes,
    *refs,
):
    given, out32, held = refs[:9], refs[9], refs[10:19]
    route_body(sizes, given, held, out32, *refs[19:])


def route_body(
    sizes,
    given,
    held,
    out32,
    insem,
    xb,
    send,
    recv,
    inbox,
    outbox,
    lat,
    base_out,
    sel,
    w_hi,
    w_lo,
    wo_hi,
    wo_lo,
    perm,
    scat,
    mask_o,
    mask_c,
    toep,
    toep_t,
    ssem,
    rsem,
    cssem,
    crsem,
):
    hours, members, regions, orders, reaches, classes, panel = sizes
    x_ref, send_rows_ref, idx_ref, w_ref, cls_ref, shape_ref, rate_ref, outlets_ref, inc_ref = held
    loads = [
        pltpu.make_async_copy(given[i], held[i], insem.at[i]) for i in range(len(held))
    ]
    for load in loads:
        load.start()
    groups = members // MG
    slots = send.shape[2] * regions
    r = lax.axis_index("region")
    o = lax.axis_index("order")
    nxt = lax.rem(o + 1, orders)
    prv = lax.rem(o + orders - 1, orders)

    barrier = pltpu.get_barrier_semaphore()

    def greet(d, c):
        peer = lax.rem(r + d, regions)
        pl.semaphore_signal(barrier, inc=1, device_id=(peer, o), device_id_type=MESH)
        return c

    lax.fori_loop(1, regions, greet, 0)
    pl.semaphore_signal(barrier, inc=1, device_id=(r, nxt), device_id_type=MESH)
    pl.semaphore_signal(barrier, inc=1, device_id=(r, prv), device_id_type=MESH)

    n0 = iota((slots, 128), 0)
    c1 = iota((slots, 128), 1)
    spread = onehot(c1 == (n0 >> 4) * 4 + (n0 & 3)).astype(BF)
    loads[1].wait()
    row_hit = onehot(send_rows_ref[...] == (iota((128, 128), 0) & 31)).astype(BF)
    picked = mm_nt(spread, row_hit)
    sel[...] = jnp.where(((n0 >> 2) & 3) == (c1 >> 5), picked, 0.0).astype(BF)
    xb[:, 128:LANES] = jnp.zeros((xb.shape[0], LANES - 128), BF)

    loads[0].wait()
    pl.semaphore_wait(barrier, regions + 1)

    def dispatch(g, c):
        rows = MG * 32
        start = pl.multiple_of(g * rows, rows)
        xb[:, 0:hours] = x_ref[pl.ds(start, rows), :].astype(BF)
        send[g] = mm(sel[...], xb[...]).astype(BF).reshape(send.shape[1:])
        pltpu.make_async_copy(send.at[g, r], recv.at[g, r], rsem.at[g]).start()

        def push(d, c):
            peer = lax.rem(r + d, regions)
            pltpu.make_async_remote_copy(
                src_ref=send.at[g, peer],
                dst_ref=recv.at[g, r],
                send_sem=ssem.at[g],
                recv_sem=rsem.at[g],
                device_id=(peer, o),
                device_id_type=MESH,
            ).start()
            return c

        return lax.fori_loop(1, regions, push, c)

    lax.fori_loop(0, groups, dispatch, 0)

    for load in loads[2:]:
        load.wait()

    diag = iota((classes, classes), 0) == iota((classes, classes), 1)
    rate = jnp.sum(
        jnp.where(diag, jnp.broadcast_to(rate_ref[...], (classes, classes)), 0.0),
        axis=1,
        keepdims=True,
    )
    lag = iota((classes, hours), 1).astype(F32)
    unit = rate * shape_ref[...] * jnp.exp(-rate * lag)
    base_out[0:classes, 128:LANES] = jnp.zeros((classes, LANES - 128), F32)
    base_out[0:classes, 0:hours] = unit.astype(BF).astype(F32)
    later = iota((LANES, LANES), 1) >= iota((LANES, LANES), 0)

    def table(k, c):
        row = jnp.broadcast_to(base_out[pl.ds(k, 1), :], (LANES, LANES))
        turned = pltpu.roll(row, 0, 1, stride=1, stride_axis=0)
        turned = jnp.where(later, turned, 0.0)
        at = pl.multiple_of(k * LANES, LANES)
        toep_t[pl.ds(at, LANES), :] = turned.astype(BF)
        toep[:, pl.ds(at, LANES)] = turned.T.astype(BF)
        return c

    lax.fori_loop(0, classes, table, 0)

    pos = (n0 >> 4) * 4 + (n0 & 3)
    weights_t = jnp.zeros((slots, 128), F32)
    for j in range(4):
        weights_t = weights_t + jnp.where(idx_ref[j : j + 1, :] == pos, w_ref[j : j + 1, :], 0.0)
    weights = weights_t.T
    high = weights.astype(BF)
    low = (weights - high.astype(F32)).astype(BF)
    member_of = (iota((reaches, slots), 1) >> 2) & 3
    for m in range(MG):
        here = onehot(member_of == m).astype(BF)
        w_hi[m * 128 : (m + 1) * 128, :] = high * here
        w_lo[m * 128 : (m + 1) * 128, :] = low * here

    i0 = iota((128, 128), 0)
    i1 = iota((128, 128), 1)
    copies = onehot((iota((128, panel), 0) & 31) == iota((128, panel), 1)).astype(BF)
    at_outlet = onehot(outlets_ref[...] == iota((reaches, panel), 0)).astype(BF)
    outlet_of = mm_nt(copies, at_outlet)
    link_of = mm(copies, inc_ref[...].astype(F32).astype(BF))
    link_t = link_of.T
    for m in range(MG):
        scat[m * 128 : (m + 1) * 128, :] = jnp.where((i1 >> 5) == m, link_t, 0.0).astype(BF)
    outlet_bf = outlet_of.astype(BF)
    own = ((iota((MG * panel, slots), 1) >> 2) & 3) == (iota((MG * panel, slots), 0) >> 5)
    wo_hi[...] = jnp.where(own, mm(outlet_bf, high), 0.0).astype(BF)
    wo_lo[...] = jnp.where(own, mm(outlet_bf, low), 0.0).astype(BF)
    joined = mm_nt(outlet_bf, link_of.astype(BF))
    perm[...] = jnp.where((i0 >> 5) == (i1 >> 5), joined, 0.0).astype(BF)
    cls_c = jnp.broadcast_to(cls_ref[...].astype(F32), (128, 128)).T
    cls_o = mm(outlet_bf, cls_c.astype(BF))
    for k in range(classes):
        hit_c = onehot(cls_c == float(k)).astype(BF)
        hit_o = onehot(cls_o == float(k)).astype(BF)
        for a in range(2):
            mask_o[k, :, a * 128 : (a + 1) * 128] = hit_o
            for b in range(2):
                mask_c[k, b * 128 : (b + 1) * 128, a * 128 : (a + 1) * 128] = hit_c

    def route(rows):
        total = mm(rows * mask_o[0], toep_t[0:LANES, :])
        for k in range(1, classes):
            total = total + mm(rows * mask_o[k], toep_t[k * LANES : (k + 1) * LANES, :])
        return total

    def group(g, c):
        pltpu.make_async_copy(recv.at[g], recv.at[g], rsem.at[g]).wait()
        got = recv[g].reshape(slots, LANES)

        def pass_on():
            pltpu.make_async_remote_copy(
                src_ref=outbox.at[g],
                dst_ref=inbox.at[g],
                send_sem=cssem.at[g],
                recv_sem=crsem.at[g],
                device_id=(r, nxt),
                device_id_type=MESH,
            ).start()

        @pl.when(o < orders - 1)
        def _():
            base_out[...] = route((mm(wo_hi[...], got) + mm(wo_lo[...], got)).astype(BF))

        @pl.when(o == 0)
        def _():
            outbox[g] = base_out[...].astype(BF)
            pass_on()

        lat[...] = mm(w_hi[...], got) + mm(w_lo[...], got)

        @pl.when(o > 0)
        def _():
            pltpu.make_async_copy(inbox.at[g], inbox.at[g], crsem.at[g]).wait()

            @pl.when(o < orders - 1)
            def _():
                moved = mm(perm[...], inbox[g]).astype(BF)
                outbox[g] = (base_out[...] + route(moved)).astype(BF)
                pass_on()

            lat[...] = lat[...] + mm(scat[...], inbox[g])

        def pair(h, c):
            entering = lat[pl.ds(pl.multiple_of(h * 256, 256), 256), :].astype(BF)
            total = mm_nt(toep[:, 0:LANES], entering * mask_c[0])
            for k in range(1, classes):
                at = k * LANES
                total = total + mm_nt(toep[:, at : at + LANES], entering * mask_c[k])
            for m in range(2):
                first = g * MG + h * 2 + m
                out32[pl.ds(first, hours, stride=members), :] = total[
                    0:hours, m * 128 : (m + 1) * 128
                ]
            return c

        return lax.fori_loop(0, 2, pair, c)

    lax.fori_loop(0, groups, group, 0)

    def drain(g, c):
        sent = send.at[g, pl.ds(0, regions - 1)]
        pltpu.make_async_copy(sent, sent, ssem.at[g]).wait()

        @pl.when(o < orders - 1)
        def _():
            pltpu.make_async_copy(outbox.at[g], outbox.at[g], cssem.at[g]).wait()

        return c

    lax.fori_loop(0, groups, drain, 0)


def local(
    regions,
    orders,
    runoff,
    send_rows,
    remap_index,
    remap_weight,
    class_id,
    kernel_shape,
    kernel_rate,
    outlets,
    incidence,
):
    hours, members, rows = runoff.shape
    reaches = remap_index.shape[0]
    classes = kernel_shape.shape[0]
    panel = outlets.shape[2]
    groups = members // MG
    slots = regions * MG * 4
    sizes = (hours, members, regions, orders, reaches, classes, panel)
    given = (
        jnp.transpose(runoff, (1, 2, 0)).reshape(members * rows, hours),
        send_rows.reshape(1, -1),
        remap_index.T,
        remap_weight.T,
        class_id.reshape(1, -1),
        kernel_shape,
        kernel_rate.reshape(1, -1),
        outlets.reshape(1, -1),
        incidence.reshape(panel, reaches),
    )
    flat = pl.pallas_call(
        functools.partial(kernel, sizes),
        out_shape=pltpu.VMEM((hours * members, reaches), F32),
        in_specs=[pl.BlockSpec(memory_space=pltpu.HBM)] * len(given),
        out_specs=pl.BlockSpec(memory_space=pltpu.VMEM),
        scratch_shapes=[pltpu.VMEM(a.shape, a.dtype) for a in given]
        + [
            pltpu.SemaphoreType.DMA((len(given),)),
            pltpu.VMEM((MG * rows, LANES), BF),
            pltpu.VMEM((groups, regions, MG * 4, LANES), BF),
            pltpu.VMEM((groups, regions, MG * 4, LANES), BF),
            pltpu.VMEM((groups, MG * panel, LANES), BF),
            pltpu.VMEM((groups, MG * panel, LANES), BF),
            pltpu.VMEM((MG * reaches, LANES), F32),
            pltpu.VMEM((MG * panel, LANES), F32),
            pltpu.VMEM((slots, MG * rows), BF),
            pltpu.VMEM((MG * reaches, slots), BF),
            pltpu.VMEM((MG * reaches, slots), BF),
            pltpu.VMEM((MG * panel, slots), BF),
            pltpu.VMEM((MG * panel, slots), BF),
            pltpu.VMEM((MG * panel, MG * panel), BF),
            pltpu.VMEM((MG * reaches, MG * panel), BF),
            pltpu.VMEM((classes, MG * panel, LANES), BF),
            pltpu.VMEM((classes, 2 * reaches, LANES), BF),
            pltpu.VMEM((LANES, classes * LANES), BF),
            pltpu.VMEM((classes * LANES, LANES), BF),
            pltpu.SemaphoreType.DMA((groups,)),
            pltpu.SemaphoreType.DMA((groups,)),
            pltpu.SemaphoreType.DMA((groups,)),
            pltpu.SemaphoreType.DMA((groups,)),
        ],
        compiler_params=pltpu.CompilerParams(
            collective_id=0, has_side_effects=True, vmem_limit_bytes=56 << 20
        ),
        name="route_levels",
    )(*given)
    return flat.reshape(hours, members, reaches).astype(BF)


def solution(mesh):
    return jax.shard_map(
        functools.partial(local, mesh.shape["region"], mesh.shape["order"]),
        mesh=mesh,
        in_specs=(
            P(None, None, ("region", "order")),
            P("region", "order", None),
            P(("region", "order"), None),
            P(("region", "order"), None),
            P(("region", "order"), None),
            P(),
            P(),
            P("region", "order", None),
            P("region", "order", None, None),
        ),
        out_specs=P(None, None, ("region", "order")),
        check_vma=False,
    )
```

```python
import functools

import jax
import jax.numpy as jnp
from jax import lax
from jax.experimental import pallas as pl
from jax.experimental.pallas import tpu as pltpu
from jax.sharding import PartitionSpec as P

MESH = pl.DeviceIdType.MESH
BF = jnp.bfloat16
NX, NZ = 4, 8
F32 = jnp.float32
LANES = 256
AHEAD = 2
PICK = 2
LAG = 4
MG = 4


def mm(a, b):
    return jnp.dot(a, b, preferred_element_type=F32)


def mm_nt(a, b):
    return lax.dot_general(a, b, (((1,), (1,)), ((), ())), preferred_element_type=F32)


def iota(shape, dim):
    return lax.broadcasted_iota(jnp.int32, shape, dim)


def onehot(hits):
    return jnp.where(hits, 1.0, 0.0)


def kernel(
    sizes,
    *refs,
):
    given, out32, held = refs[:9], refs[9], refs[10:19]
    route_body(sizes, given, held, out32, *refs[19:])


def route_body(
    sizes,
    given,
    held,
    out32,
    insem,
    own,
    near1,
    near2,
    meta,
    send_n,
    send_f,
    recv,
    inbox,
    outbox,
    lat,
    base_out,
    sel,
    w_hi,
    w_lo,
    wo_hi,
    wo_lo,
    perm,
    scat,
    mask_o,
    mask_c,
    toep,
    toep_t,
    msend,
    mrecv,
    s1s,
    s1r,
    s2s,
    s2r,
    nsem,
    fsem,
    rsem,
    cssem,
    crsem,
):
    hours, members, regions, orders, reaches, classes, panel = sizes
    x_ref, send_rows_ref, idx_ref, w_ref, cls_ref, shape_ref, rate_ref, outlets_ref, inc_ref = held
    loads = [
        pltpu.make_async_copy(given[i], held[i], insem.at[i]) for i in range(len(held))
    ]
    for load in loads:
        load.start()
    groups = members // MG
    slots = regions * MG * 4
    r = lax.axis_index("region")
    o = lax.axis_index("order")
    x = r // NZ
    z = lax.rem(r, NZ)
    nxt = lax.rem(o + 1, orders)
    prv = lax.rem(o + orders - 1, orders)

    def at(dx, dz):
        return (lax.rem(x + dx + NX, NX) * NZ + lax.rem(z + dz + NZ, NZ), o)

    barrier = pltpu.get_barrier_semaphore()

    def greet(n, c):
        peer = at(n // 5, lax.rem(n, 5) + NZ - 2)
        pl.semaphore_signal(barrier, inc=1, device_id=peer, device_id_type=MESH)
        return c

    lax.fori_loop(0, 2, greet, 0)
    lax.fori_loop(3, NX * 5, greet, 0)
    pl.semaphore_signal(barrier, inc=1, device_id=(r, prv), device_id_type=MESH)

    own[:, :, 128:LANES] = jnp.zeros((groups, MG * 32, LANES - 128), BF)
    loads[0].wait()

    def cast(g, c):
        rows = MG * 32
        start = pl.multiple_of(g * rows, rows)
        own[g, :, 0:hours] = x_ref[pl.ds(start, rows), :].astype(BF)
        return c

    lax.fori_loop(0, groups, cast, 0)
    loads[1].wait()
    meta[2] = send_rows_ref[...]
    pl.semaphore_wait(barrier, NX * 5)

    def step1(g):
        for way in range(2):
            pltpu.make_async_remote_copy(
                src_ref=own.at[g],
                dst_ref=near1.at[g, way],
                send_sem=s1s.at[g, way],
                recv_sem=s1r.at[g, way],
                device_id=at(0, 1 - 2 * way),
                device_id_type=MESH,
            ).start()

    def step2(g):
        for way in range(2):
            pltpu.make_async_copy(near1.at[g, way], near1.at[g, way], s1r.at[g, way]).wait()
            pltpu.make_async_remote_copy(
                src_ref=near1.at[g, way],
                dst_ref=near2.at[g, way],
                send_sem=s2s.at[g, way],
                recv_sem=s2r.at[g, way],
                device_id=at(0, 1 - 2 * way),
                device_id_type=MESH,
            ).start()

    step1(0)
    tell = [
        pltpu.make_async_remote_copy(
            src_ref=send_rows_ref,
            dst_ref=meta.at[2 + dz],
            send_sem=msend.at[n],
            recv_sem=mrecv.at[2 + dz],
            device_id=at(0, dz),
            device_id_type=MESH,
        )
        for n, dz in enumerate((1, -1, 2, -2))
    ]
    for copy in tell:
        copy.start()
    for g in range(1, AHEAD):
        step1(g)
    for load in loads[2:]:
        load.wait()

    diag = iota((classes, classes), 0) == iota((classes, classes), 1)
    rate = jnp.sum(
        jnp.where(diag, jnp.broadcast_to(rate_ref[...], (classes, classes)), 0.0),
        axis=1,
        keepdims=True,
    )
    lag = iota((classes, hours), 1).astype(F32)
    unit = rate * shape_ref[...] * jnp.exp(-rate * lag)
    base_out[0:classes, 128:LANES] = jnp.zeros((classes, LANES - 128), F32)
    base_out[0:classes, 0:hours] = unit.astype(BF).astype(F32)
    later = iota((LANES, LANES), 1) >= iota((LANES, LANES), 0)

    def table(k, c):
        row = jnp.broadcast_to(base_out[pl.ds(k, 1), :], (LANES, LANES))
        turned = pltpu.roll(row, 0, 1, stride=1, stride_axis=0)
        turned = jnp.where(later, turned, 0.0)
        at = pl.multiple_of(k * LANES, LANES)
        toep_t[pl.ds(at, LANES), :] = turned.astype(BF)
        toep[:, pl.ds(at, LANES)] = turned.T.astype(BF)
        return c

    lax.fori_loop(0, classes, table, 0)

    n0 = iota((slots, 128), 0)
    source = (n0 >> 7) * NZ + ((z + 2 + NZ - ((n0 >> 4) & 7)) & 7)
    pos = source * 4 + (n0 & 3)
    weights_t = jnp.zeros((slots, 128), F32)
    for j in range(4):
        weights_t = weights_t + jnp.where(idx_ref[j : j + 1, :] == pos, w_ref[j : j + 1, :], 0.0)
    weights = weights_t.T
    high = weights.astype(BF)
    low = (weights - high.astype(F32)).astype(BF)
    member_of = (iota((reaches, slots), 1) >> 2) & 3
    for m in range(MG):
        here = onehot(member_of == m).astype(BF)
        w_hi[m * 128 : (m + 1) * 128, :] = high * here
        w_lo[m * 128 : (m + 1) * 128, :] = low * here

    i0 = iota((128, 128), 0)
    i1 = iota((128, 128), 1)
    copies = onehot((iota((128, panel), 0) & 31) == iota((128, panel), 1)).astype(BF)
    at_outlet = onehot(outlets_ref[...] == iota((reaches, panel), 0)).astype(BF)
    outlet_of = mm_nt(copies, at_outlet)
    link_of = mm(copies, inc_ref[...].astype(F32).astype(BF))
    link_t = link_of.T
    for m in range(MG):
        scat[m * 128 : (m + 1) * 128, :] = jnp.where((i1 >> 5) == m, link_t, 0.0).astype(BF)
    outlet_bf = outlet_of.astype(BF)
    mine = ((iota((MG * panel, slots), 1) >> 2) & 3) == (iota((MG * panel, slots), 0) >> 5)
    wo_hi[...] = jnp.where(mine, mm(outlet_bf, high), 0.0).astype(BF)
    wo_lo[...] = jnp.where(mine, mm(outlet_bf, low), 0.0).astype(BF)
    joined = mm_nt(outlet_bf, link_of.astype(BF))
    perm[...] = jnp.where((i0 >> 5) == (i1 >> 5), joined, 0.0).astype(BF)
    cls_c = jnp.broadcast_to(cls_ref[...].astype(F32), (128, 128)).T
    cls_o = mm(outlet_bf, cls_c.astype(BF))
    for k in range(classes):
        hit_c = onehot(cls_c == float(k)).astype(BF)
        hit_o = onehot(cls_o == float(k)).astype(BF)
        for a in range(2):
            mask_o[k, :, a * 128 : (a + 1) * 128] = hit_o
            for b in range(2):
                mask_c[k, b * 128 : (b + 1) * 128, a * 128 : (a + 1) * 128] = hit_c

    for copy in tell:
        copy.wait_recv()
    k0 = iota((160, 128), 0)
    k1 = iota((160, 128), 1)
    part = k0 >> 6
    for e in range(5):
        way = 1 if e < 2 else 0
        ahead = part * (1 - 2 * way)
        to_x = jnp.where(part == 2, (x + 2 * way + ((k0 >> 4) & 3)) & 3, (k0 >> 4) & 3)
        to_z = (z + ahead + NZ) & 7
        spread = onehot(k1 == (to_x * NZ + to_z) * 4 + (k0 & 3)).astype(BF)
        row_hit = onehot(meta[e] == (iota((128, 128), 0) & 31)).astype(BF)
        picked = mm_nt(spread, row_hit)
        sel[e] = jnp.where(((k0 >> 2) & 3) == (k1 >> 5), picked, 0.0).astype(BF)

    def select(g):
        for way in range(2):
            pltpu.make_async_copy(near2.at[g, way], near2.at[g, way], s2r.at[g, way]).wait()
        held_blocks = (near2[g, 1], near1[g, 1], own[g], near1[g, 0], near2[g, 0])
        for e in (0, 4, 1, 2, 3):
            outer = e == 0 or e == 4
            taken = mm(sel[e] if outer else sel[e, 0:64, :], held_blocks[e]).astype(BF)
            send_n[g, :, e] = taken[0:64].reshape(NX, MG * 4, LANES)
            if outer:
                way = 0 if e == 4 else 1
                send_f[g, way] = taken[64:160].reshape(6, MG * 4, LANES)

                def far(n, c, way=way):
                    two = n // 4
                    dx = n + two * (2 * way)
                    dz = (1 + two) * (1 - 2 * way)
                    to_x = jnp.where(two == 1, lax.rem(x + dx, NX), n)
                    peer = (to_x * NZ + lax.rem(z + dz + NZ, NZ), o)
                    into = jnp.where(two == 1, 6, 5 + 2 * way)
                    pltpu.make_async_remote_copy(
                        src_ref=send_f.at[g, way, n],
                        dst_ref=recv.at[g, x, into],
                        send_sem=fsem.at[g],
                        recv_sem=rsem.at[g],
                        device_id=peer,
                        device_id_type=MESH,
                    ).start()
                    return c

                lax.fori_loop(0, 6, far, 0)

        def near(d, c):
            to_x = lax.rem(x + d, NX)
            pltpu.make_async_remote_copy(
                src_ref=send_n.at[g, to_x],
                dst_ref=recv.at[g, x, pl.ds(0, 5)],
                send_sem=nsem.at[g],
                recv_sem=rsem.at[g],
                device_id=(to_x * NZ + z, o),
                device_id_type=MESH,
            ).start()
            return c

        lax.fori_loop(1, NX, near, 0)
        pltpu.make_async_copy(send_n.at[g, x], recv.at[g, x, pl.ds(0, 5)], rsem.at[g]).start()

    def route(rows):
        wide = jnp.concatenate([rows * mask_o[k] for k in range(classes)], axis=1)
        return mm(wide, toep_t[...])

    def group(g):
        pltpu.make_async_copy(recv.at[g], recv.at[g], rsem.at[g]).wait()
        got = recv[g].reshape(slots, LANES)

        def pass_on():
            pltpu.make_async_remote_copy(
                src_ref=outbox.at[g],
                dst_ref=inbox.at[g],
                send_sem=cssem.at[g],
                recv_sem=crsem.at[g],
                device_id=(r, nxt),
                device_id_type=MESH,
            ).start()

        @pl.when(o < orders - 1)
        def _():
            base_out[...] = route((mm(wo_hi[...], got) + mm(wo_lo[...], got)).astype(BF))

        @pl.when(o == 0)
        def _():
            outbox[g] = base_out[...].astype(BF)
            pass_on()

        lat[...] = mm(w_hi[...], got) + mm(w_lo[...], got)

        @pl.when(o > 0)
        def _():
            pltpu.make_async_copy(inbox.at[g], inbox.at[g], crsem.at[g]).wait()

            @pl.when(o < orders - 1)
            def _():
                moved = mm(perm[...], inbox[g]).astype(BF)
                outbox[g] = (base_out[...] + route(moved)).astype(BF)
                pass_on()

            lat[...] = lat[...] + mm(scat[...], inbox[g])

        def pair(h, c):
            entering = lat[pl.ds(pl.multiple_of(h * 256, 256), 256), :].astype(BF)
            wide = jnp.concatenate([entering * mask_c[k] for k in range(classes)], axis=1)
            total = mm_nt(toep[...], wide)
            for m in range(2):
                first = g * MG + h * 2 + m
                out32[pl.ds(first, hours, stride=members), :] = total[
                    0:hours, m * 128 : (m + 1) * 128
                ]
            return c

        lax.fori_loop(0, 2, pair, 0)

    def turn(i, c):
        @pl.when(i < groups - AHEAD)
        def _():
            step1(i + AHEAD)

        @pl.when(i < groups)
        def _():
            step2(i)

        @pl.when(jnp.logical_and(i >= PICK, i < groups + PICK))
        def _():
            select(i - PICK)

        @pl.when(i >= LAG)
        def _():
            group(i - LAG)

        return c

    lax.fori_loop(0, groups + LAG, turn, 0)

    for copy in tell:
        copy.wait_send()

    def drain(g, c):
        for way in range(2):
            pltpu.make_async_copy(own.at[g], own.at[g], s1s.at[g, way]).wait()
            pltpu.make_async_copy(near1.at[g, way], near1.at[g, way], s2s.at[g, way]).wait()
        sent = send_n.at[g, pl.ds(0, NX - 1)]
        pltpu.make_async_copy(sent, sent, nsem.at[g]).wait()
        pltpu.make_async_copy(send_f.at[g], send_f.at[g], fsem.at[g]).wait()

        @pl.when(o < orders - 1)
        def _():
            pltpu.make_async_copy(outbox.at[g], outbox.at[g], cssem.at[g]).wait()

        return c

    lax.fori_loop(0, groups, drain, 0)


def local(
    regions,
    orders,
    runoff,
    send_rows,
    remap_index,
    remap_weight,
    class_id,
    kernel_shape,
    kernel_rate,
    outlets,
    incidence,
):
    hours, members, rows = runoff.shape
    reaches = remap_index.shape[0]
    classes = kernel_shape.shape[0]
    panel = outlets.shape[2]
    groups = members // MG
    slots = regions * MG * 4
    sizes = (hours, members, regions, orders, reaches, classes, panel)
    given = (
        jnp.transpose(runoff, (1, 2, 0)).reshape(members * rows, hours),
        send_rows.reshape(1, -1),
        remap_index.T,
        remap_weight.T,
        class_id.reshape(1, -1),
        kernel_shape,
        kernel_rate.reshape(1, -1),
        outlets.reshape(1, -1),
        incidence.reshape(panel, reaches),
    )
    flat = pl.pallas_call(
        functools.partial(kernel, sizes),
        out_shape=pltpu.VMEM((hours * members, reaches), F32),
        in_specs=[pl.BlockSpec(memory_space=pltpu.HBM)] * len(given),
        out_specs=pl.BlockSpec(memory_space=pltpu.VMEM),
        scratch_shapes=[pltpu.VMEM(a.shape, a.dtype) for a in given]
        + [
            pltpu.SemaphoreType.DMA((len(given),)),
            pltpu.VMEM((groups, MG * rows, LANES), BF),
            pltpu.VMEM((groups, 2, MG * rows, LANES), BF),
            pltpu.VMEM((groups, 2, MG * rows, LANES), BF),
            pltpu.VMEM((5, 1, 128), jnp.int32),
            pltpu.VMEM((groups, NX, 5, MG * 4, LANES), BF),
            pltpu.VMEM((groups, 2, 6, MG * 4, LANES), BF),
            pltpu.VMEM((groups, NX, NZ, MG * 4, LANES), BF),
            pltpu.VMEM((groups, MG * panel, LANES), BF),
            pltpu.VMEM((groups, MG * panel, LANES), BF),
            pltpu.VMEM((MG * reaches, LANES), F32),
            pltpu.VMEM((MG * panel, LANES), F32),
            pltpu.VMEM((5, 160, MG * rows), BF),
            pltpu.VMEM((MG * reaches, slots), BF),
            pltpu.VMEM((MG * reaches, slots), BF),
            pltpu.VMEM((MG * panel, slots), BF),
            pltpu.VMEM((MG * panel, slots), BF),
            pltpu.VMEM((MG * panel, MG * panel), BF),
            pltpu.VMEM((MG * reaches, MG * panel), BF),
            pltpu.VMEM((classes, MG * panel, LANES), BF),
            pltpu.VMEM((classes, 2 * reaches, LANES), BF),
            pltpu.VMEM((LANES, classes * LANES), BF),
            pltpu.VMEM((classes * LANES, LANES), BF),
            pltpu.SemaphoreType.DMA((4,)),
            pltpu.SemaphoreType.DMA((5,)),
            pltpu.SemaphoreType.DMA((groups, 2)),
            pltpu.SemaphoreType.DMA((groups, 2)),
            pltpu.SemaphoreType.DMA((groups, 2)),
            pltpu.SemaphoreType.DMA((groups, 2)),
            pltpu.SemaphoreType.DMA((groups,)),
            pltpu.SemaphoreType.DMA((groups,)),
            pltpu.SemaphoreType.DMA((groups,)),
            pltpu.SemaphoreType.DMA((groups,)),
            pltpu.SemaphoreType.DMA((groups,)),
        ],
        compiler_params=pltpu.CompilerParams(
            collective_id=0, has_side_effects=True, vmem_limit_bytes=56 << 20
        ),
        name="route_levels",
    )(*given)
    return flat.reshape(hours, members, reaches).astype(BF)


def solution(mesh):
    return jax.shard_map(
        functools.partial(local, mesh.shape["region"], mesh.shape["order"]),
        mesh=mesh,
        in_specs=(
            P(None, None, ("region", "order")),
            P("region", "order", None),
            P(("region", "order"), None),
            P(("region", "order"), None),
            P(("region", "order"), None),
            P(),
            P(),
            P("region", "order", None),
            P("region", "order", None, None),
        ),
        out_specs=P(None, None, ("region", "order")),
        check_vma=False,
    )
```

```python
import functools

import jax
import jax.numpy as jnp
from jax import lax
from jax.experimental import pallas as pl
from jax.experimental.pallas import tpu as pltpu
from jax.sharding import PartitionSpec as P

MESH = pl.DeviceIdType.MESH
BF = jnp.bfloat16
NX, NZ = 4, 8
F32 = jnp.float32
LANES = 256
AHEAD = 2
SPARE = 14
PICK = 2
LAG = 4
MG = 4


def mm(a, b):
    return jnp.dot(a, b, preferred_element_type=F32)


def mm_nt(a, b):
    return lax.dot_general(a, b, (((1,), (1,)), ((), ())), preferred_element_type=F32)


def iota(shape, dim):
    return lax.broadcasted_iota(jnp.int32, shape, dim)


def onehot(hits):
    return jnp.where(hits, 1.0, 0.0)


def kernel(
    sizes,
    *refs,
):
    given, out32, held = refs[:9], refs[9], refs[10:19]
    route_body(sizes, given, held, out32, *refs[19:])


def route_body(
    sizes,
    given,
    held,
    out32,
    insem,
    own,
    near1,
    near2,
    meta,
    send_n,
    send_f,
    recv,
    inbox,
    outbox,
    lat,
    base_out,
    sel,
    w_hi,
    w_lo,
    wo_hi,
    wo_lo,
    perm,
    scat,
    mask_o,
    mask_c,
    toep,
    toep_t,
    msend,
    mrecv,
    s1s,
    s1r,
    s2s,
    s2r,
    nsem,
    fsem,
    rsem,
    cssem,
    crsem,
):
    hours, members, regions, orders, reaches, classes, panel = sizes
    x_ref, send_rows_ref, idx_ref, w_ref, cls_ref, shape_ref, rate_ref, outlets_ref, inc_ref = held
    loads = [
        pltpu.make_async_copy(given[i], held[i], insem.at[i]) for i in range(len(held))
    ]
    for load in loads:
        load.start()
    groups = members // MG
    slots = regions * MG * 4
    r = lax.axis_index("region")
    o = lax.axis_index("order")
    x = r // NZ
    z = lax.rem(r, NZ)
    nxt = lax.rem(o + 1, orders)
    prv = lax.rem(o + orders - 1, orders)

    def at(dx, dz):
        return (lax.rem(x + dx + NX, NX) * NZ + lax.rem(z + dz + NZ, NZ), o)

    barrier = pltpu.get_barrier_semaphore()

    def greet(n, c):
        peer = at(n // 5, lax.rem(n, 5) + NZ - 2)
        pl.semaphore_signal(barrier, inc=1, device_id=peer, device_id_type=MESH)
        return c

    lax.fori_loop(0, 2, greet, 0)
    lax.fori_loop(3, NX * 5, greet, 0)
    pl.semaphore_signal(barrier, inc=1, device_id=(r, prv), device_id_type=MESH)

    own[:, :, 128:LANES] = jnp.zeros((groups, MG * 32, LANES - 128), BF)
    loads[0].wait()

    def cast(g, c):
        rows = MG * 32
        start = pl.multiple_of(g * rows, rows)
        own[g, :, 0:hours] = x_ref[pl.ds(start, rows), :].astype(BF)
        return c

    lax.fori_loop(0, groups, cast, 0)
    loads[1].wait()
    meta[2] = send_rows_ref[...]
    pl.semaphore_wait(barrier, NX * 5)

    def step1(g):
        for way in range(2):
            pltpu.make_async_remote_copy(
                src_ref=own.at[g],
                dst_ref=near1.at[g, way],
                send_sem=s1s.at[g, way],
                recv_sem=s1r.at[g, way],
                device_id=at(0, 1 - 2 * way),
                device_id_type=MESH,
            ).start()

    def step2(g):
        for way in range(2):
            pltpu.make_async_copy(near1.at[g, way], near1.at[g, way], s1r.at[g, way]).wait()
            pltpu.make_async_remote_copy(
                src_ref=near1.at[g, way],
                dst_ref=near2.at[g, way],
                send_sem=s2s.at[g, way],
                recv_sem=s2r.at[g, way],
                device_id=at(0, 1 - 2 * way),
                device_id_type=MESH,
            ).start()

    step1(0)
    tell = [
        pltpu.make_async_remote_copy(
            src_ref=send_rows_ref,
            dst_ref=meta.at[2 + dz],
            send_sem=msend.at[n],
            recv_sem=mrecv.at[2 + dz],
            device_id=at(0, dz),
            device_id_type=MESH,
        )
        for n, dz in enumerate((1, -1, 2, -2))
    ]
    for copy in tell:
        copy.start()
    for g in range(1, AHEAD):
        step1(g)
    for load in loads[2:]:
        load.wait()

    diag = iota((classes, classes), 0) == iota((classes, classes), 1)
    rate = jnp.sum(
        jnp.where(diag, jnp.broadcast_to(rate_ref[...], (classes, classes)), 0.0),
        axis=1,
        keepdims=True,
    )
    lag = iota((classes, hours), 1).astype(F32)
    unit = rate * shape_ref[...] * jnp.exp(-rate * lag)
    base_out[0:classes, 128:LANES] = jnp.zeros((classes, LANES - 128), F32)
    base_out[0:classes, 0:hours] = unit.astype(BF).astype(F32)
    later = iota((LANES, LANES), 1) >= iota((LANES, LANES), 0)

    def table(k, c):
        row = jnp.broadcast_to(base_out[pl.ds(k, 1), :], (LANES, LANES))
        turned = pltpu.roll(row, 0, 1, stride=1, stride_axis=0)
        turned = jnp.where(later, turned, 0.0)
        at = pl.multiple_of(k * LANES, LANES)
        toep_t[pl.ds(at, LANES), :] = turned.astype(BF)
        flipped = turned.T.astype(BF)
        here = pl.multiple_of(k * 128, 128)
        toep[:, pl.ds(here, 128)] = flipped[:, 0:128]
        toep[:, pl.ds(here + classes * 128, 128)] = flipped[:, 128:LANES]
        return c

    lax.fori_loop(0, classes, table, 0)

    n0 = iota((slots, 128), 0)
    source = (n0 >> 7) * NZ + ((z + 2 + NZ - ((n0 >> 4) & 7)) & 7)
    pos = source * 4 + (n0 & 3)
    weights_t = jnp.zeros((slots, 128), F32)
    for j in range(4):
        weights_t = weights_t + jnp.where(idx_ref[j : j + 1, :] == pos, w_ref[j : j + 1, :], 0.0)
    weights = weights_t.T
    high = weights.astype(BF)
    low = (weights - high.astype(F32)).astype(BF)
    member_of = (iota((reaches, slots), 1) >> 2) & 3
    for m in range(MG):
        here = onehot(member_of == m).astype(BF)
        w_hi[m * 128 : (m + 1) * 128, :] = high * here
        w_lo[m * 128 : (m + 1) * 128, :] = low * here

    i0 = iota((128, 128), 0)
    i1 = iota((128, 128), 1)
    copies = onehot((iota((128, panel), 0) & 31) == iota((128, panel), 1)).astype(BF)
    at_outlet = onehot(outlets_ref[...] == iota((reaches, panel), 0)).astype(BF)
    outlet_of = mm_nt(copies, at_outlet)
    link_of = mm(copies, inc_ref[...].astype(F32).astype(BF))
    link_t = link_of.T
    for m in range(MG):
        scat[m * 128 : (m + 1) * 128, :] = jnp.where((i1 >> 5) == m, link_t, 0.0).astype(BF)
    outlet_bf = outlet_of.astype(BF)
    mine = ((iota((MG * panel, slots), 1) >> 2) & 3) == (iota((MG * panel, slots), 0) >> 5)
    wo_hi[...] = jnp.where(mine, mm(outlet_bf, high), 0.0).astype(BF)
    wo_lo[...] = jnp.where(mine, mm(outlet_bf, low), 0.0).astype(BF)
    joined = mm_nt(outlet_bf, link_of.astype(BF))
    perm[...] = jnp.where((i0 >> 5) == (i1 >> 5), joined, 0.0).astype(BF)
    cls_c = jnp.broadcast_to(cls_ref[...].astype(F32), (128, 128)).T
    cls_o = mm(outlet_bf, cls_c.astype(BF))
    for k in range(classes):
        hit_c = onehot(cls_c == float(k)).astype(BF)
        hit_o = onehot(cls_o == float(k)).astype(BF)
        for a in range(2):
            mask_o[k, :, a * 128 : (a + 1) * 128] = hit_o
            mask_c[k, a * 128 : (a + 1) * 128, :] = hit_c

    for copy in tell:
        copy.wait_recv()
    k0 = iota((160, 128), 0)
    k1 = iota((160, 128), 1)
    part = k0 >> 6
    for e in range(5):
        way = 1 if e < 2 else 0
        ahead = part * (1 - 2 * way)
        to_x = jnp.where(part == 2, (x + 2 * way + ((k0 >> 4) & 3)) & 3, (k0 >> 4) & 3)
        to_z = (z + ahead + NZ) & 7
        spread = onehot(k1 == (to_x * NZ + to_z) * 4 + (k0 & 3)).astype(BF)
        row_hit = onehot(meta[e] == (iota((128, 128), 0) & 31)).astype(BF)
        picked = mm_nt(spread, row_hit)
        sel[e] = jnp.where(((k0 >> 2) & 3) == (k1 >> 5), picked, 0.0).astype(BF)

    def select(g):
        for way in range(2):
            pltpu.make_async_copy(near2.at[g, way], near2.at[g, way], s2r.at[g, way]).wait()
        held_blocks = (near2[g, 1], near1[g, 1], own[g], near1[g, 0], near2[g, 0])
        for e in (0, 4, 1, 2, 3):
            outer = e == 0 or e == 4
            taken = mm(sel[e] if outer else sel[e, 0:64, :], held_blocks[e]).astype(BF)
            send_n[g, :, e] = taken[0:64].reshape(NX, MG * 4, LANES)
            if outer:
                way = 0 if e == 4 else 1
                send_f[g, way] = taken[64:160].reshape(6, MG * 4, LANES)

                def far(n, c, way=way):
                    two = n // 4
                    dx = n + two * (2 * way)
                    dz = (1 + two) * (1 - 2 * way)
                    to_x = jnp.where(two == 1, lax.rem(x + dx, NX), n)
                    peer = (to_x * NZ + lax.rem(z + dz + NZ, NZ), o)
                    into = jnp.where(two == 1, 6, 5 + 2 * way)
                    pltpu.make_async_remote_copy(
                        src_ref=send_f.at[g, way, n],
                        dst_ref=recv.at[g, x, into],
                        send_sem=fsem.at[g],
                        recv_sem=rsem.at[g],
                        device_id=peer,
                        device_id_type=MESH,
                    ).start()
                    return c

                lax.fori_loop(0, 6, far, 0)

        def near(d, c):
            to_x = lax.rem(x + d, NX)
            pltpu.make_async_remote_copy(
                src_ref=send_n.at[g, to_x],
                dst_ref=recv.at[g, x, pl.ds(0, 5)],
                send_sem=nsem.at[g],
                recv_sem=rsem.at[g],
                device_id=(to_x * NZ + z, o),
                device_id_type=MESH,
            ).start()
            return c

        lax.fori_loop(1, NX, near, 0)
        pltpu.make_async_copy(send_n.at[g, x], recv.at[g, x, pl.ds(0, 5)], rsem.at[g]).start()

    def route(rows):
        wide = jnp.concatenate([rows * mask_o[k] for k in range(classes)], axis=1)
        return mm(wide, toep_t[...])

    def intake(g):
        pltpu.make_async_copy(recv.at[g], recv.at[g], rsem.at[g]).wait()
        got = recv[g].reshape(slots, LANES)

        @pl.when(o < orders - 1)
        def _():
            base_out[...] = route((mm(wo_hi[...], got) + mm(wo_lo[...], got)).astype(BF))

        @pl.when(o == 0)
        def _():
            outbox[g] = base_out[...].astype(BF)
            pass_on(g)

        lat[g] = mm(w_hi[...], got) + mm(w_lo[...], got)

    def pass_on(g):
        pltpu.make_async_remote_copy(
            src_ref=outbox.at[g],
            dst_ref=inbox.at[g],
            send_sem=cssem.at[g],
            recv_sem=crsem.at[g],
            device_id=(r, nxt),
            device_id_type=MESH,
        ).start()

    def level(g):
        @pl.when(o > 0)
        def _():
            pltpu.make_async_copy(inbox.at[g], inbox.at[g], crsem.at[g]).wait()

        @pl.when(jnp.logical_and(o > 0, o < orders - 1))
        def _():
            moved = mm(perm[...], inbox[g]).astype(BF)
            outbox[g] = (base_out[...] + route(moved)).astype(BF)
            pass_on(g)

    def total(g):
        @pl.when(o > 0)
        def _():
            lat[g] = lat[g] + mm(scat[...], inbox[g])

        def pair(h, c):
            entering = lat[g, pl.ds(pl.multiple_of(h * 256, 256), 256), :].astype(BF)
            early, late_in = [
                jnp.concatenate([entering[:, h : h + 128] * mask_c[k] for k in range(classes)], axis=1)
                for h in (0, 128)
            ]
            flow = mm_nt(toep[:, 0 : classes * 128], early)
            tail = mm_nt(toep[128:LANES, classes * 128 :], late_in)
            for m in range(2):
                first = g * MG + h * 2 + m
                cols = slice(m * 128, (m + 1) * 128)
                out32[pl.ds(first, 128, stride=members), :] = flow[0:128, cols]
                out32[pl.ds(first + 128 * members, hours - 128, stride=members), :] = (
                    flow[128:hours, cols] + tail[0 : hours - 128, cols]
                )
            return c

        lax.fori_loop(0, 2, pair, 0)

    late = jnp.minimum(groups, (orders - 1 - o) * SPARE // (orders - 1))

    lag = LAG + o // 3

    def turn(i, c):
        @pl.when(i < groups - AHEAD)
        def _():
            step1(i + AHEAD)

        @pl.when(i < groups)
        def _():
            step2(i)

        @pl.when(jnp.logical_and(i >= PICK, i < groups + PICK))
        def _():
            select(i - PICK)

        @pl.when(jnp.logical_and(i >= lag, i < groups + lag))
        def _():
            intake(i - lag)
            level(i - lag)

            @pl.when(i - lag < groups - late)
            def _():
                total(i - lag)

        return c

    lax.fori_loop(0, groups + LAG + 2, turn, 0)

    def rest(g, c):
        total(g)
        return c

    lax.fori_loop(groups - late, groups, rest, 0)

    for copy in tell:
        copy.wait_send()

    def drain(g, c):
        for way in range(2):
            pltpu.make_async_copy(own.at[g], own.at[g], s1s.at[g, way]).wait()
            pltpu.make_async_copy(near1.at[g, way], near1.at[g, way], s2s.at[g, way]).wait()
        sent = send_n.at[g, pl.ds(0, NX - 1)]
        pltpu.make_async_copy(sent, sent, nsem.at[g]).wait()
        pltpu.make_async_copy(send_f.at[g], send_f.at[g], fsem.at[g]).wait()

        @pl.when(o < orders - 1)
        def _():
            pltpu.make_async_copy(outbox.at[g], outbox.at[g], cssem.at[g]).wait()

        return c

    lax.fori_loop(0, groups, drain, 0)


def local(
    regions,
    orders,
    runoff,
    send_rows,
    remap_index,
    remap_weight,
    class_id,
    kernel_shape,
    kernel_rate,
    outlets,
    incidence,
):
    hours, members, rows = runoff.shape
    reaches = remap_index.shape[0]
    classes = kernel_shape.shape[0]
    panel = outlets.shape[2]
    groups = members // MG
    slots = regions * MG * 4
    sizes = (hours, members, regions, orders, reaches, classes, panel)
    given = (
        jnp.transpose(runoff, (1, 2, 0)).reshape(members * rows, hours),
        send_rows.reshape(1, -1),
        remap_index.T,
        remap_weight.T,
        class_id.reshape(1, -1),
        kernel_shape,
        kernel_rate.reshape(1, -1),
        outlets.reshape(1, -1),
        incidence.reshape(panel, reaches),
    )
    flat = pl.pallas_call(
        functools.partial(kernel, sizes),
        out_shape=pltpu.VMEM((hours * members, reaches), F32),
        in_specs=[pl.BlockSpec(memory_space=pltpu.HBM)] * len(given),
        out_specs=pl.BlockSpec(memory_space=pltpu.VMEM),
        scratch_shapes=[pltpu.VMEM(a.shape, a.dtype) for a in given]
        + [
            pltpu.SemaphoreType.DMA((len(given),)),
            pltpu.VMEM((groups, MG * rows, LANES), BF),
            pltpu.VMEM((groups, 2, MG * rows, LANES), BF),
            pltpu.VMEM((groups, 2, MG * rows, LANES), BF),
            pltpu.VMEM((5, 1, 128), jnp.int32),
            pltpu.VMEM((groups, NX, 5, MG * 4, LANES), BF),
            pltpu.VMEM((groups, 2, 6, MG * 4, LANES), BF),
            pltpu.VMEM((groups, NX, NZ, MG * 4, LANES), BF),
            pltpu.VMEM((groups, MG * panel, LANES), BF),
            pltpu.VMEM((groups, MG * panel, LANES), BF),
            pltpu.VMEM((groups, MG * reaches, LANES), F32),
            pltpu.VMEM((MG * panel, LANES), F32),
            pltpu.VMEM((5, 160, MG * rows), BF),
            pltpu.VMEM((MG * reaches, slots), BF),
            pltpu.VMEM((MG * reaches, slots), BF),
            pltpu.VMEM((MG * panel, slots), BF),
            pltpu.VMEM((MG * panel, slots), BF),
            pltpu.VMEM((MG * panel, MG * panel), BF),
            pltpu.VMEM((MG * reaches, MG * panel), BF),
            pltpu.VMEM((classes, MG * panel, LANES), BF),
            pltpu.VMEM((classes, 2 * reaches, 128), BF),
            pltpu.VMEM((LANES, classes * LANES), BF),
            pltpu.VMEM((classes * LANES, LANES), BF),
            pltpu.SemaphoreType.DMA((4,)),
            pltpu.SemaphoreType.DMA((5,)),
            pltpu.SemaphoreType.DMA((groups, 2)),
            pltpu.SemaphoreType.DMA((groups, 2)),
            pltpu.SemaphoreType.DMA((groups, 2)),
            pltpu.SemaphoreType.DMA((groups, 2)),
            pltpu.SemaphoreType.DMA((groups,)),
            pltpu.SemaphoreType.DMA((groups,)),
            pltpu.SemaphoreType.DMA((groups,)),
            pltpu.SemaphoreType.DMA((groups,)),
            pltpu.SemaphoreType.DMA((groups,)),
        ],
        compiler_params=pltpu.CompilerParams(
            collective_id=0, has_side_effects=True, vmem_limit_bytes=56 << 20
        ),
        name="route_levels",
    )(*given)
    return flat.reshape(hours, members, reaches).astype(BF)


def solution(mesh):
    return jax.shard_map(
        functools.partial(local, mesh.shape["region"], mesh.shape["order"]),
        mesh=mesh,
        in_specs=(
            P(None, None, ("region", "order")),
            P("region", "order", None),
            P(("region", "order"), None),
            P(("region", "order"), None),
            P(("region", "order"), None),
            P(),
            P(),
            P("region", "order", None),
            P("region", "order", None, None),
        ),
        out_specs=P(None, None, ("region", "order")),
        check_vma=False,
    )
```

```python
import functools

import jax
import jax.numpy as jnp
from jax import lax
from jax.experimental import pallas as pl
from jax.experimental.pallas import tpu as pltpu
from jax.sharding import PartitionSpec as P

MESH = pl.DeviceIdType.MESH
BF = jnp.bfloat16
NX, NZ = 4, 8
F32 = jnp.float32
LANES = 256
AHEAD = 2
SPARE = 14
PICK = 2
LAG = 4
MG = 4


def mm(a, b):
    return jnp.dot(a, b, preferred_element_type=F32)


def mm_nt(a, b):
    return lax.dot_general(a, b, (((1,), (1,)), ((), ())), preferred_element_type=F32)


def iota(shape, dim):
    return lax.broadcasted_iota(jnp.int32, shape, dim)


def onehot(hits):
    return jnp.where(hits, 1.0, 0.0)


def kernel(
    sizes,
    *refs,
):
    given, out32, held = refs[:9], refs[9], refs[10:19]
    route_body(sizes, given, held, out32, *refs[19:])


def route_body(
    sizes,
    given,
    held,
    out32,
    insem,
    turn_buf,
    own,
    near1,
    near2,
    meta,
    send_n,
    send_f,
    recv,
    inbox,
    outbox,
    lat,
    base_out,
    sel,
    w_hi,
    w_lo,
    wo_hi,
    wo_lo,
    perm,
    scat,
    mask_o,
    mask_c,
    toep,
    toep_t,
    msend,
    mrecv,
    s1s,
    s1r,
    s2s,
    s2r,
    nsem,
    fsem,
    rsem,
    cssem,
    crsem,
):
    hours, members, regions, orders, reaches, classes, panel = sizes
    x_ref, send_rows_ref, idx_ref, w_ref, cls_ref, shape_ref, rate_ref, outlets_ref, inc_ref = held
    loads = [
        pltpu.make_async_copy(given[i], held[i], insem.at[i]) for i in range(len(held))
    ]
    for load in loads:
        load.start()
    groups = members // MG
    slots = regions * MG * 4
    r = lax.axis_index("region")
    o = lax.axis_index("order")
    x = r // NZ
    z = lax.rem(r, NZ)
    nxt = lax.rem(o + 1, orders)
    prv = lax.rem(o + orders - 1, orders)

    def at(dx, dz):
        return (lax.rem(x + dx + NX, NX) * NZ + lax.rem(z + dz + NZ, NZ), o)

    barrier = pltpu.get_barrier_semaphore()

    def greet(n, c):
        peer = at(n // 5, lax.rem(n, 5) + NZ - 2)
        pl.semaphore_signal(barrier, inc=1, device_id=peer, device_id_type=MESH)
        return c

    lax.fori_loop(0, 2, greet, 0)
    lax.fori_loop(3, NX * 5, greet, 0)
    pl.semaphore_signal(barrier, inc=1, device_id=(r, prv), device_id_type=MESH)

    filler = jnp.zeros((groups, 2, LANES - hours, 128), BF)
    near1[:, :, hours:LANES] = filler
    near2[:, :, hours:LANES] = filler
    turn_buf[...] = jnp.zeros_like(turn_buf)
    loads[0].wait()

    def cast(g, c):
        rows = MG * 32
        start = pl.multiple_of(g * rows, rows)
        own[g, 0:128] = x_ref[pl.ds(start, rows), 0:128].astype(BF)
        turn_buf[:, 0 : hours - 128] = x_ref[pl.ds(start, rows), 128:hours]
        own[g, 128:LANES] = turn_buf[...].T.astype(BF)
        return c

    lax.fori_loop(0, groups, cast, 0)
    loads[1].wait()
    meta[2] = send_rows_ref[...]
    pl.semaphore_wait(barrier, NX * 5)

    def step1(g):
        for way in range(2):
            pltpu.make_async_remote_copy(
                src_ref=own.at[g, pl.ds(0, hours)],
                dst_ref=near1.at[g, way, pl.ds(0, hours)],
                send_sem=s1s.at[g, way],
                recv_sem=s1r.at[g, way],
                device_id=at(0, 1 - 2 * way),
                device_id_type=MESH,
            ).start()

    def step2(g):
        for way in range(2):
            got = near1.at[g, way, pl.ds(0, hours)]
            pltpu.make_async_copy(got, got, s1r.at[g, way]).wait()
            pltpu.make_async_remote_copy(
                src_ref=got,
                dst_ref=near2.at[g, way, pl.ds(0, hours)],
                send_sem=s2s.at[g, way],
                recv_sem=s2r.at[g, way],
                device_id=at(0, 1 - 2 * way),
                device_id_type=MESH,
            ).start()

    step1(0)
    tell = [
        pltpu.make_async_remote_copy(
            src_ref=send_rows_ref,
            dst_ref=meta.at[2 + dz],
            send_sem=msend.at[n],
            recv_sem=mrecv.at[2 + dz],
            device_id=at(0, dz),
            device_id_type=MESH,
        )
        for n, dz in enumerate((1, -1, 2, -2))
    ]
    for copy in tell:
        copy.start()
    for g in range(1, AHEAD):
        step1(g)
    for load in loads[2:]:
        load.wait()

    diag = iota((classes, classes), 0) == iota((classes, classes), 1)
    rate = jnp.sum(
        jnp.where(diag, jnp.broadcast_to(rate_ref[...], (classes, classes)), 0.0),
        axis=1,
        keepdims=True,
    )
    lag = iota((classes, hours), 1).astype(F32)
    unit = rate * shape_ref[...] * jnp.exp(-rate * lag)
    base_out[0:classes, 128:LANES] = jnp.zeros((classes, LANES - 128), F32)
    base_out[0:classes, 0:hours] = unit.astype(BF).astype(F32)
    later = iota((LANES, LANES), 1) >= iota((LANES, LANES), 0)

    def table(k, c):
        row = jnp.broadcast_to(base_out[pl.ds(k, 1), :], (LANES, LANES))
        turned = pltpu.roll(row, 0, 1, stride=1, stride_axis=0)
        turned = jnp.where(later, turned, 0.0)
        at = pl.multiple_of(k * LANES, LANES)
        toep_t[pl.ds(at, LANES), :] = turned.astype(BF)
        flipped = turned.T.astype(BF)
        here = pl.multiple_of(k * 128, 128)
        toep[:, pl.ds(here, 128)] = flipped[:, 0:128]
        toep[:, pl.ds(here + classes * 128, 128)] = flipped[:, 128:LANES]
        return c

    lax.fori_loop(0, classes, table, 0)

    n0 = iota((slots, 128), 0)
    source = (n0 >> 7) * NZ + ((z + 2 + NZ - ((n0 >> 4) & 7)) & 7)
    pos = source * 4 + (n0 & 3)
    weights_t = jnp.zeros((slots, 128), F32)
    for j in range(4):
        weights_t = weights_t + jnp.where(idx_ref[j : j + 1, :] == pos, w_ref[j : j + 1, :], 0.0)
    weights = weights_t.T
    high = weights.astype(BF)
    low = (weights - high.astype(F32)).astype(BF)
    member_of = (iota((reaches, slots), 1) >> 2) & 3
    for m in range(MG):
        here = onehot(member_of == m).astype(BF)
        w_hi[m * 128 : (m + 1) * 128, :] = high * here
        w_lo[m * 128 : (m + 1) * 128, :] = low * here

    i0 = iota((128, 128), 0)
    i1 = iota((128, 128), 1)
    copies = onehot((iota((128, panel), 0) & 31) == iota((128, panel), 1)).astype(BF)
    at_outlet = onehot(outlets_ref[...] == iota((reaches, panel), 0)).astype(BF)
    outlet_of = mm_nt(copies, at_outlet)
    link_of = mm(copies, inc_ref[...].astype(F32).astype(BF))
    link_t = link_of.T
    for m in range(MG):
        scat[m * 128 : (m + 1) * 128, :] = jnp.where((i1 >> 5) == m, link_t, 0.0).astype(BF)
    outlet_bf = outlet_of.astype(BF)
    mine = ((iota((MG * panel, slots), 1) >> 2) & 3) == (iota((MG * panel, slots), 0) >> 5)
    wo_hi[...] = jnp.where(mine, mm(outlet_bf, high), 0.0).astype(BF)
    wo_lo[...] = jnp.where(mine, mm(outlet_bf, low), 0.0).astype(BF)
    joined = mm_nt(outlet_bf, link_of.astype(BF))
    perm[...] = jnp.where((i0 >> 5) == (i1 >> 5), joined, 0.0).astype(BF)
    cls_c = jnp.broadcast_to(cls_ref[...].astype(F32), (128, 128)).T
    cls_o = mm(outlet_bf, cls_c.astype(BF))
    for k in range(classes):
        hit_c = onehot(cls_c == float(k)).astype(BF)
        hit_o = onehot(cls_o == float(k)).astype(BF)
        for a in range(2):
            mask_o[k, :, a * 128 : (a + 1) * 128] = hit_o
            mask_c[k, a * 128 : (a + 1) * 128, :] = hit_c

    for copy in tell:
        copy.wait_recv()
    k0 = iota((160, 128), 0)
    k1 = iota((160, 128), 1)
    part = k0 >> 6
    for e in range(5):
        way = 1 if e < 2 else 0
        ahead = part * (1 - 2 * way)
        to_x = jnp.where(part == 2, (x + 2 * way + ((k0 >> 4) & 3)) & 3, (k0 >> 4) & 3)
        to_z = (z + ahead + NZ) & 7
        spread = onehot(k1 == (to_x * NZ + to_z) * 4 + (k0 & 3)).astype(BF)
        row_hit = onehot(meta[e] == (iota((128, 128), 0) & 31)).astype(BF)
        picked = mm_nt(spread, row_hit)
        sel[e] = jnp.where(((k0 >> 2) & 3) == (k1 >> 5), picked, 0.0).astype(BF)

    def select(g):
        for way in range(2):
            got = near2.at[g, way, pl.ds(0, hours)]
            pltpu.make_async_copy(got, got, s2r.at[g, way]).wait()
        held_blocks = (near2[g, 1], near1[g, 1], own[g], near1[g, 0], near2[g, 0])
        for e in (0, 4, 1, 2, 3):
            outer = e == 0 or e == 4
            pick = sel[e] if outer else sel[e, 0:64, :]
            block = held_blocks[e]
            taken = jnp.concatenate(
                [mm(pick, block[0:128]), mm_nt(pick, block[128:LANES])], axis=1
            ).astype(BF)
            send_n[g, :, e] = taken[0:64].reshape(NX, MG * 4, LANES)
            if outer:
                way = 0 if e == 4 else 1
                send_f[g, way] = taken[64:160].reshape(6, MG * 4, LANES)

                def far(n, c, way=way):
                    two = n // 4
                    dx = n + two * (2 * way)
                    dz = (1 + two) * (1 - 2 * way)
                    to_x = jnp.where(two == 1, lax.rem(x + dx, NX), n)
                    peer = (to_x * NZ + lax.rem(z + dz + NZ, NZ), o)
                    into = jnp.where(two == 1, 6, 5 + 2 * way)
                    pltpu.make_async_remote_copy(
                        src_ref=send_f.at[g, way, n],
                        dst_ref=recv.at[g, x, into],
                        send_sem=fsem.at[g],
                        recv_sem=rsem.at[g],
                        device_id=peer,
                        device_id_type=MESH,
                    ).start()
                    return c

                lax.fori_loop(0, 6, far, 0)

        def near(d, c):
            to_x = lax.rem(x + d, NX)
            pltpu.make_async_remote_copy(
                src_ref=send_n.at[g, to_x],
                dst_ref=recv.at[g, x, pl.ds(0, 5)],
                send_sem=nsem.at[g],
                recv_sem=rsem.at[g],
                device_id=(to_x * NZ + z, o),
                device_id_type=MESH,
            ).start()
            return c

        lax.fori_loop(1, NX, near, 0)
        pltpu.make_async_copy(send_n.at[g, x], recv.at[g, x, pl.ds(0, 5)], rsem.at[g]).start()

    def route(rows):
        wide = jnp.concatenate([rows * mask_o[k] for k in range(classes)], axis=1)
        return mm(wide, toep_t[...])

    def intake(g):
        pltpu.make_async_copy(recv.at[g], recv.at[g], rsem.at[g]).wait()
        got = recv[g].reshape(slots, LANES)

        @pl.when(o < orders - 1)
        def _():
            base_out[...] = route((mm(wo_hi[...], got) + mm(wo_lo[...], got)).astype(BF))

        @pl.when(o == 0)
        def _():
            outbox[g] = base_out[...].astype(BF)
            pass_on(g)

        lat[g] = mm(w_hi[...], got) + mm(w_lo[...], got)

    def pass_on(g):
        pltpu.make_async_remote_copy(
            src_ref=outbox.at[g],
            dst_ref=inbox.at[g],
            send_sem=cssem.at[g],
            recv_sem=crsem.at[g],
            device_id=(r, nxt),
            device_id_type=MESH,
        ).start()

    def level(g):
        @pl.when(o > 0)
        def _():
            pltpu.make_async_copy(inbox.at[g], inbox.at[g], crsem.at[g]).wait()

        @pl.when(jnp.logical_and(o > 0, o < orders - 1))
        def _():
            moved = mm(perm[...], inbox[g]).astype(BF)
            outbox[g] = (base_out[...] + route(moved)).astype(BF)
            pass_on(g)

    def total(g):
        @pl.when(o > 0)
        def _():
            lat[g] = lat[g] + mm(scat[...], inbox[g])

        def pair(h, c):
            entering = lat[g, pl.ds(pl.multiple_of(h * 256, 256), 256), :].astype(BF)
            early, late_in = [
                jnp.concatenate([entering[:, h : h + 128] * mask_c[k] for k in range(classes)], axis=1)
                for h in (0, 128)
            ]
            flow = mm_nt(toep[:, 0 : classes * 128], early)
            tail = mm_nt(toep[128:LANES, classes * 128 :], late_in)
            for m in range(2):
                first = g * MG + h * 2 + m
                cols = slice(m * 128, (m + 1) * 128)
                out32[pl.ds(first, 128, stride=members), :] = flow[0:128, cols]
                out32[pl.ds(first + 128 * members, hours - 128, stride=members), :] = (
                    flow[128:hours, cols] + tail[0 : hours - 128, cols]
                )
            return c

        lax.fori_loop(0, 2, pair, 0)

    late = jnp.minimum(groups, (orders - 1 - o) * SPARE // (orders - 1))

    lag = LAG + o // 3

    def turn(i, c):
        @pl.when(i < groups - AHEAD)
        def _():
            step1(i + AHEAD)

        @pl.when(i < groups)
        def _():
            step2(i)

        @pl.when(jnp.logical_and(i >= PICK, i < groups + PICK))
        def _():
            select(i - PICK)

        @pl.when(jnp.logical_and(i >= lag, i < groups + lag))
        def _():
            intake(i - lag)
            level(i - lag)

            @pl.when(i - lag < groups - late)
            def _():
                total(i - lag)

        return c

    lax.fori_loop(0, groups + LAG + 2, turn, 0)

    def rest(g, c):
        total(g)
        return c

    lax.fori_loop(groups - late, groups, rest, 0)

    for copy in tell:
        copy.wait_send()

    def drain(g, c):
        for way in range(2):
            mine, passed = own.at[g, pl.ds(0, hours)], near1.at[g, way, pl.ds(0, hours)]
            pltpu.make_async_copy(mine, mine, s1s.at[g, way]).wait()
            pltpu.make_async_copy(passed, passed, s2s.at[g, way]).wait()
        sent = send_n.at[g, pl.ds(0, NX - 1)]
        pltpu.make_async_copy(sent, sent, nsem.at[g]).wait()
        pltpu.make_async_copy(send_f.at[g], send_f.at[g], fsem.at[g]).wait()

        @pl.when(o < orders - 1)
        def _():
            pltpu.make_async_copy(outbox.at[g], outbox.at[g], cssem.at[g]).wait()

        return c

    lax.fori_loop(0, groups, drain, 0)


def local(
    regions,
    orders,
    runoff,
    send_rows,
    remap_index,
    remap_weight,
    class_id,
    kernel_shape,
    kernel_rate,
    outlets,
    incidence,
):
    hours, members, rows = runoff.shape
    reaches = remap_index.shape[0]
    classes = kernel_shape.shape[0]
    panel = outlets.shape[2]
    groups = members // MG
    slots = regions * MG * 4
    sizes = (hours, members, regions, orders, reaches, classes, panel)
    given = (
        jnp.transpose(runoff, (1, 2, 0)).reshape(members * rows, hours),
        send_rows.reshape(1, -1),
        remap_index.T,
        remap_weight.T,
        class_id.reshape(1, -1),
        kernel_shape,
        kernel_rate.reshape(1, -1),
        outlets.reshape(1, -1),
        incidence.reshape(panel, reaches),
    )
    flat = pl.pallas_call(
        functools.partial(kernel, sizes),
        out_shape=pltpu.VMEM((hours * members, reaches), F32),
        in_specs=[pl.BlockSpec(memory_space=pltpu.HBM)] * len(given),
        out_specs=pl.BlockSpec(memory_space=pltpu.VMEM),
        scratch_shapes=[pltpu.VMEM(a.shape, a.dtype) for a in given]
        + [
            pltpu.SemaphoreType.DMA((len(given),)),
            pltpu.VMEM((MG * rows, 128), F32),
            pltpu.VMEM((groups, LANES, MG * rows), BF),
            pltpu.VMEM((groups, 2, LANES, MG * rows), BF),
            pltpu.VMEM((groups, 2, LANES, MG * rows), BF),
            pltpu.VMEM((5, 1, 128), jnp.int32),
            pltpu.VMEM((groups, NX, 5, MG * 4, LANES), BF),
            pltpu.VMEM((groups, 2, 6, MG * 4, LANES), BF),
            pltpu.VMEM((groups, NX, NZ, MG * 4, LANES), BF),
            pltpu.VMEM((groups, MG * panel, LANES), BF),
            pltpu.VMEM((groups, MG * panel, LANES), BF),
            pltpu.VMEM((groups, MG * reaches, LANES), F32),
            pltpu.VMEM((MG * panel, LANES), F32),
            pltpu.VMEM((5, 160, MG * rows), BF),
            pltpu.VMEM((MG * reaches, slots), BF),
            pltpu.VMEM((MG * reaches, slots), BF),
            pltpu.VMEM((MG * panel, slots), BF),
            pltpu.VMEM((MG * panel, slots), BF),
            pltpu.VMEM((MG * panel, MG * panel), BF),
            pltpu.VMEM((MG * reaches, MG * panel), BF),
            pltpu.VMEM((classes, MG * panel, LANES), BF),
            pltpu.VMEM((classes, 2 * reaches, 128), BF),
            pltpu.VMEM((LANES, classes * LANES), BF),
            pltpu.VMEM((classes * LANES, LANES), BF),
            pltpu.SemaphoreType.DMA((4,)),
            pltpu.SemaphoreType.DMA((5,)),
            pltpu.SemaphoreType.DMA((groups, 2)),
            pltpu.SemaphoreType.DMA((groups, 2)),
            pltpu.SemaphoreType.DMA((groups, 2)),
            pltpu.SemaphoreType.DMA((groups, 2)),
            pltpu.SemaphoreType.DMA((groups,)),
            pltpu.SemaphoreType.DMA((groups,)),
            pltpu.SemaphoreType.DMA((groups,)),
            pltpu.SemaphoreType.DMA((groups,)),
            pltpu.SemaphoreType.DMA((groups,)),
        ],
        compiler_params=pltpu.CompilerParams(
            collective_id=0, has_side_effects=True, vmem_limit_bytes=56 << 20
        ),
        name="route_levels",
    )(*given)
    return flat.reshape(hours, members, reaches).astype(BF)


def solution(mesh):
    return jax.shard_map(
        functools.partial(local, mesh.shape["region"], mesh.shape["order"]),
        mesh=mesh,
        in_specs=(
            P(None, None, ("region", "order")),
            P("region", "order", None),
            P(("region", "order"), None),
            P(("region", "order"), None),
            P(("region", "order"), None),
            P(),
            P(),
            P("region", "order", None),
            P("region", "order", None, None),
        ),
        out_specs=P(None, None, ("region", "order")),
        check_vma=False,
    )
```

```python
import functools

import jax
import jax.numpy as jnp
from jax import lax
from jax.experimental import pallas as pl
from jax.experimental.pallas import tpu as pltpu
from jax.sharding import PartitionSpec as P

MESH = pl.DeviceIdType.MESH
BF = jnp.bfloat16
NX, NZ = 4, 8
F32 = jnp.float32
LANES = 256
AHEAD = 2
SPARE = 14
PICK = 2
LAG = 4
MG = 4


def mm(a, b):
    return jnp.dot(a, b, preferred_element_type=F32)


def mm_nt(a, b):
    return lax.dot_general(a, b, (((1,), (1,)), ((), ())), preferred_element_type=F32)


def iota(shape, dim):
    return lax.broadcasted_iota(jnp.int32, shape, dim)


def onehot(hits):
    return jnp.where(hits, 1.0, 0.0)


def kernel(
    sizes,
    *refs,
):
    given, out32, held = refs[:9], refs[9], refs[10:19]
    route_body(sizes, given, held, out32, *refs[19:])


def route_body(
    sizes,
    given,
    held,
    out32,
    insem,
    turn_buf,
    own,
    near1,
    near2,
    meta,
    send_n,
    send_f,
    recv,
    inbox,
    outbox,
    lat,
    base_out,
    sel,
    w_hi,
    w_lo,
    wo_hi,
    wo_lo,
    perm,
    scat,
    mask_o,
    mask_c,
    toep,
    toep_t,
    msend,
    mrecv,
    s1s,
    s1r,
    s2s,
    s2r,
    nsem,
    fsem,
    rsem,
    cssem,
    crsem,
):
    hours, members, regions, orders, reaches, classes, panel = sizes
    x_ref, send_rows_ref, idx_ref, w_ref, cls_ref, shape_ref, rate_ref, outlets_ref, inc_ref = held
    groups = members // MG
    soon = AHEAD * MG * 32
    parts = (pl.ds(0, soon), pl.ds(soon, groups * MG * 32 - soon))
    loads = [pltpu.make_async_copy(given[0].at[parts[0]], x_ref.at[parts[0]], insem.at[0])] + [
        pltpu.make_async_copy(given[i], held[i], insem.at[i]) for i in range(1, len(held))
    ]
    others = pltpu.make_async_copy(given[0].at[parts[1]], x_ref.at[parts[1]], insem.at[len(held)])
    for load in loads[:2] + [others] + loads[2:]:
        load.start()
    slots = regions * MG * 4
    r = lax.axis_index("region")
    o = lax.axis_index("order")
    x = r // NZ
    z = lax.rem(r, NZ)
    nxt = lax.rem(o + 1, orders)
    prv = lax.rem(o + orders - 1, orders)

    def at(dx, dz):
        return (lax.rem(x + dx + NX, NX) * NZ + lax.rem(z + dz + NZ, NZ), o)

    barrier = pltpu.get_barrier_semaphore()

    def greet(n, c):
        peer = at(n // 5, lax.rem(n, 5) + NZ - 2)
        pl.semaphore_signal(barrier, inc=1, device_id=peer, device_id_type=MESH)
        return c

    lax.fori_loop(0, 2, greet, 0)
    lax.fori_loop(3, NX * 5, greet, 0)
    pl.semaphore_signal(barrier, inc=1, device_id=(r, prv), device_id_type=MESH)

    filler = jnp.zeros((groups, 2, LANES - hours, 128), BF)
    near1[:, :, hours:LANES] = filler
    near2[:, :, hours:LANES] = filler
    turn_buf[...] = jnp.zeros_like(turn_buf)
    loads[0].wait()

    def cast(g, c):
        rows = MG * 32
        start = pl.multiple_of(g * rows, rows)
        own[g, 0:128] = x_ref[pl.ds(start, rows), 0:128].astype(BF)
        turn_buf[:, 0 : hours - 128] = x_ref[pl.ds(start, rows), 128:hours]
        own[g, 128:LANES] = turn_buf[...].T.astype(BF)
        return c

    lax.fori_loop(0, AHEAD, cast, 0)
    loads[1].wait()
    meta[2] = send_rows_ref[...]
    pl.semaphore_wait(barrier, NX * 5)

    def step1(g):
        for way in range(2):
            pltpu.make_async_remote_copy(
                src_ref=own.at[g, pl.ds(0, hours)],
                dst_ref=near1.at[g, way, pl.ds(0, hours)],
                send_sem=s1s.at[g, way],
                recv_sem=s1r.at[g, way],
                device_id=at(0, 1 - 2 * way),
                device_id_type=MESH,
            ).start()

    def step2(g):
        for way in range(2):
            got = near1.at[g, way, pl.ds(0, hours)]
            pltpu.make_async_copy(got, got, s1r.at[g, way]).wait()
            pltpu.make_async_remote_copy(
                src_ref=got,
                dst_ref=near2.at[g, way, pl.ds(0, hours)],
                send_sem=s2s.at[g, way],
                recv_sem=s2r.at[g, way],
                device_id=at(0, 1 - 2 * way),
                device_id_type=MESH,
            ).start()

    step1(0)
    tell = [
        pltpu.make_async_remote_copy(
            src_ref=send_rows_ref,
            dst_ref=meta.at[2 + dz],
            send_sem=msend.at[n],
            recv_sem=mrecv.at[2 + dz],
            device_id=at(0, dz),
            device_id_type=MESH,
        )
        for n, dz in enumerate((1, -1, 2, -2))
    ]
    for copy in tell:
        copy.start()
    for g in range(1, AHEAD):
        step1(g)
    others.wait()
    lax.fori_loop(AHEAD, groups, cast, 0)
    for load in loads[2:]:
        load.wait()

    diag = iota((classes, classes), 0) == iota((classes, classes), 1)
    rate = jnp.sum(
        jnp.where(diag, jnp.broadcast_to(rate_ref[...], (classes, classes)), 0.0),
        axis=1,
        keepdims=True,
    )
    lag = iota((classes, hours), 1).astype(F32)
    unit = rate * shape_ref[...] * jnp.exp(-rate * lag)
    base_out[0:classes, 128:LANES] = jnp.zeros((classes, LANES - 128), F32)
    base_out[0:classes, 0:hours] = unit.astype(BF).astype(F32)
    later = iota((LANES, LANES), 1) >= iota((LANES, LANES), 0)

    def table(k, c):
        row = jnp.broadcast_to(base_out[pl.ds(k, 1), :], (LANES, LANES))
        turned = pltpu.roll(row, 0, 1, stride=1, stride_axis=0)
        turned = jnp.where(later, turned, 0.0)
        at = pl.multiple_of(k * LANES, LANES)
        toep_t[pl.ds(at, LANES), :] = turned.astype(BF)
        flipped = turned.T.astype(BF)
        here = pl.multiple_of(k * 128, 128)
        toep[:, pl.ds(here, 128)] = flipped[:, 0:128]
        toep[:, pl.ds(here + classes * 128, 128)] = flipped[:, 128:LANES]
        return c

    lax.fori_loop(0, classes, table, 0)

    n0 = iota((slots, 128), 0)
    source = (n0 >> 7) * NZ + ((z + 2 + NZ - ((n0 >> 4) & 7)) & 7)
    pos = source * 4 + (n0 & 3)
    weights_t = jnp.zeros((slots, 128), F32)
    for j in range(4):
        weights_t = weights_t + jnp.where(idx_ref[j : j + 1, :] == pos, w_ref[j : j + 1, :], 0.0)
    weights = weights_t.T
    high = weights.astype(BF)
    low = (weights - high.astype(F32)).astype(BF)
    member_of = (iota((reaches, slots), 1) >> 2) & 3
    for m in range(MG):
        here = onehot(member_of == m).astype(BF)
        w_hi[m * 128 : (m + 1) * 128, :] = high * here
        w_lo[m * 128 : (m + 1) * 128, :] = low * here

    i0 = iota((128, 128), 0)
    i1 = iota((128, 128), 1)
    copies = onehot((iota((128, panel), 0) & 31) == iota((128, panel), 1)).astype(BF)
    at_outlet = onehot(outlets_ref[...] == iota((reaches, panel), 0)).astype(BF)
    outlet_of = mm_nt(copies, at_outlet)
    link_of = mm(copies, inc_ref[...].astype(F32).astype(BF))
    link_t = link_of.T
    for m in range(MG):
        scat[m * 128 : (m + 1) * 128, :] = jnp.where((i1 >> 5) == m, link_t, 0.0).astype(BF)
    outlet_bf = outlet_of.astype(BF)
    mine = ((iota((MG * panel, slots), 1) >> 2) & 3) == (iota((MG * panel, slots), 0) >> 5)
    wo_hi[...] = jnp.where(mine, mm(outlet_bf, high), 0.0).astype(BF)
    wo_lo[...] = jnp.where(mine, mm(outlet_bf, low), 0.0).astype(BF)
    joined = mm_nt(outlet_bf, link_of.astype(BF))
    perm[...] = jnp.where((i0 >> 5) == (i1 >> 5), joined, 0.0).astype(BF)
    cls_c = jnp.broadcast_to(cls_ref[...].astype(F32), (128, 128)).T
    cls_o = mm(outlet_bf, cls_c.astype(BF))
    for k in range(classes):
        hit_c = onehot(cls_c == float(k)).astype(BF)
        hit_o = onehot(cls_o == float(k)).astype(BF)
        for a in range(2):
            mask_o[k, :, a * 128 : (a + 1) * 128] = hit_o
            mask_c[k, a * 128 : (a + 1) * 128, :] = hit_c

    for copy in tell:
        copy.wait_recv()
    k0 = iota((160, 128), 0)
    k1 = iota((160, 128), 1)
    part = k0 >> 6
    for e in range(5):
        way = 1 if e < 2 else 0
        ahead = part * (1 - 2 * way)
        to_x = jnp.where(part == 2, (x + 2 * way + ((k0 >> 4) & 3)) & 3, (k0 >> 4) & 3)
        to_z = (z + ahead + NZ) & 7
        spread = onehot(k1 == (to_x * NZ + to_z) * 4 + (k0 & 3)).astype(BF)
        row_hit = onehot(meta[e] == (iota((128, 128), 0) & 31)).astype(BF)
        picked = mm_nt(spread, row_hit)
        sel[e] = jnp.where(((k0 >> 2) & 3) == (k1 >> 5), picked, 0.0).astype(BF)

    def select(g):
        for way in range(2):
            got = near2.at[g, way, pl.ds(0, hours)]
            pltpu.make_async_copy(got, got, s2r.at[g, way]).wait()
        held_blocks = (near2[g, 1], near1[g, 1], own[g], near1[g, 0], near2[g, 0])
        for e in (0, 4, 1, 2, 3):
            outer = e == 0 or e == 4
            pick = sel[e] if outer else sel[e, 0:64, :]
            block = held_blocks[e]
            taken = jnp.concatenate(
                [mm(pick, block[0:128]), mm_nt(pick, block[128:LANES])], axis=1
            ).astype(BF)
            send_n[g, :, e] = taken[0:64].reshape(NX, MG * 4, LANES)
            if outer:
                way = 0 if e == 4 else 1
                send_f[g, way] = taken[64:160].reshape(6, MG * 4, LANES)

                def far(n, c, way=way):
                    two = n // 4
                    dx = n + two * (2 * way)
                    dz = (1 + two) * (1 - 2 * way)
                    to_x = jnp.where(two == 1, lax.rem(x + dx, NX), n)
                    peer = (to_x * NZ + lax.rem(z + dz + NZ, NZ), o)
                    into = jnp.where(two == 1, 6, 5 + 2 * way)
                    pltpu.make_async_remote_copy(
                        src_ref=send_f.at[g, way, n],
                        dst_ref=recv.at[g, x, into],
                        send_sem=fsem.at[g],
                        recv_sem=rsem.at[g],
                        device_id=peer,
                        device_id_type=MESH,
                    ).start()
                    return c

                lax.fori_loop(0, 6, far, 0)

        def near(d, c):
            to_x = lax.rem(x + d, NX)
            pltpu.make_async_remote_copy(
                src_ref=send_n.at[g, to_x],
                dst_ref=recv.at[g, x, pl.ds(0, 5)],
                send_sem=nsem.at[g],
                recv_sem=rsem.at[g],
                device_id=(to_x * NZ + z, o),
                device_id_type=MESH,
            ).start()
            return c

        lax.fori_loop(1, NX, near, 0)
        pltpu.make_async_copy(send_n.at[g, x], recv.at[g, x, pl.ds(0, 5)], rsem.at[g]).start()

    def route(rows):
        wide = jnp.concatenate([rows * mask_o[k] for k in range(classes)], axis=1)
        return mm(wide, toep_t[...])

    def intake(g):
        pltpu.make_async_copy(recv.at[g], recv.at[g], rsem.at[g]).wait()
        got = recv[g].reshape(slots, LANES)

        @pl.when(o < orders - 1)
        def _():
            base_out[...] = route((mm(wo_hi[...], got) + mm(wo_lo[...], got)).astype(BF))

        @pl.when(o == 0)
        def _():
            outbox[g] = base_out[...].astype(BF)
            pass_on(g)

        lat[g] = mm(w_hi[...], got) + mm(w_lo[...], got)

    def pass_on(g):
        pltpu.make_async_remote_copy(
            src_ref=outbox.at[g],
            dst_ref=inbox.at[g],
            send_sem=cssem.at[g],
            recv_sem=crsem.at[g],
            device_id=(r, nxt),
            device_id_type=MESH,
        ).start()

    def level(g):
        @pl.when(o > 0)
        def _():
            pltpu.make_async_copy(inbox.at[g], inbox.at[g], crsem.at[g]).wait()

        @pl.when(jnp.logical_and(o > 0, o < orders - 1))
        def _():
            moved = mm(perm[...], inbox[g]).astype(BF)
            outbox[g] = (base_out[...] + route(moved)).astype(BF)
            pass_on(g)

    def total(g):
        @pl.when(o > 0)
        def _():
            lat[g] = lat[g] + mm(scat[...], inbox[g])

        def pair(h, c):
            entering = lat[g, pl.ds(pl.multiple_of(h * 256, 256), 256), :].astype(BF)
            early, late_in = [
                jnp.concatenate([entering[:, h : h + 128] * mask_c[k] for k in range(classes)], axis=1)
                for h in (0, 128)
            ]
            flow = mm_nt(toep[:, 0 : classes * 128], early)
            tail = mm_nt(toep[128:LANES, classes * 128 :], late_in)
            for m in range(2):
                first = g * MG + h * 2 + m
                cols = slice(m * 128, (m + 1) * 128)
                out32[pl.ds(first, 128, stride=members), :] = flow[0:128, cols]
                out32[pl.ds(first + 128 * members, hours - 128, stride=members), :] = (
                    flow[128:hours, cols] + tail[0 : hours - 128, cols]
                )
            return c

        lax.fori_loop(0, 2, pair, 0)

    late = jnp.minimum(groups, (orders - 1 - o) * SPARE // (orders - 1))

    lag = LAG + o // 3

    def turn(i, c):
        @pl.when(i < groups - AHEAD)
        def _():
            step1(i + AHEAD)

        @pl.when(i < groups)
        def _():
            step2(i)

        @pl.when(jnp.logical_and(i >= PICK, i < groups + PICK))
        def _():
            select(i - PICK)

        @pl.when(jnp.logical_and(i >= lag, i < groups + lag))
        def _():
            intake(i - lag)
            level(i - lag)

            @pl.when(i - lag < groups - late)
            def _():
                total(i - lag)

        return c

    lax.fori_loop(0, groups + LAG + 2, turn, 0)

    def rest(g, c):
        total(g)
        return c

    lax.fori_loop(groups - late, groups, rest, 0)

    for copy in tell:
        copy.wait_send()

    def drain(g, c):
        for way in range(2):
            mine, passed = own.at[g, pl.ds(0, hours)], near1.at[g, way, pl.ds(0, hours)]
            pltpu.make_async_copy(mine, mine, s1s.at[g, way]).wait()
            pltpu.make_async_copy(passed, passed, s2s.at[g, way]).wait()
        sent = send_n.at[g, pl.ds(0, NX - 1)]
        pltpu.make_async_copy(sent, sent, nsem.at[g]).wait()
        pltpu.make_async_copy(send_f.at[g], send_f.at[g], fsem.at[g]).wait()

        @pl.when(o < orders - 1)
        def _():
            pltpu.make_async_copy(outbox.at[g], outbox.at[g], cssem.at[g]).wait()

        return c

    lax.fori_loop(0, groups, drain, 0)


def local(
    regions,
    orders,
    runoff,
    send_rows,
    remap_index,
    remap_weight,
    class_id,
    kernel_shape,
    kernel_rate,
    outlets,
    incidence,
):
    hours, members, rows = runoff.shape
    reaches = remap_index.shape[0]
    classes = kernel_shape.shape[0]
    panel = outlets.shape[2]
    groups = members // MG
    slots = regions * MG * 4
    sizes = (hours, members, regions, orders, reaches, classes, panel)
    given = (
        jnp.transpose(runoff, (1, 2, 0)).reshape(members * rows, hours),
        send_rows.reshape(1, -1),
        remap_index.T,
        remap_weight.T,
        class_id.reshape(1, -1),
        kernel_shape,
        kernel_rate.reshape(1, -1),
        outlets.reshape(1, -1),
        incidence.reshape(panel, reaches),
    )
    flat = pl.pallas_call(
        functools.partial(kernel, sizes),
        out_shape=pltpu.VMEM((hours * members, reaches), F32),
        in_specs=[pl.BlockSpec(memory_space=pltpu.HBM)] * len(given),
        out_specs=pl.BlockSpec(memory_space=pltpu.VMEM),
        scratch_shapes=[pltpu.VMEM(a.shape, a.dtype) for a in given]
        + [
            pltpu.SemaphoreType.DMA((len(given) + 1,)),
            pltpu.VMEM((MG * rows, 128), F32),
            pltpu.VMEM((groups, LANES, MG * rows), BF),
            pltpu.VMEM((groups, 2, LANES, MG * rows), BF),
            pltpu.VMEM((groups, 2, LANES, MG * rows), BF),
            pltpu.VMEM((5, 1, 128), jnp.int32),
            pltpu.VMEM((groups, NX, 5, MG * 4, LANES), BF),
            pltpu.VMEM((groups, 2, 6, MG * 4, LANES), BF),
            pltpu.VMEM((groups, NX, NZ, MG * 4, LANES), BF),
            pltpu.VMEM((groups, MG * panel, LANES), BF),
            pltpu.VMEM((groups, MG * panel, LANES), BF),
            pltpu.VMEM((groups, MG * reaches, LANES), F32),
            pltpu.VMEM((MG * panel, LANES), F32),
            pltpu.VMEM((5, 160, MG * rows), BF),
            pltpu.VMEM((MG * reaches, slots), BF),
            pltpu.VMEM((MG * reaches, slots), BF),
            pltpu.VMEM((MG * panel, slots), BF),
            pltpu.VMEM((MG * panel, slots), BF),
            pltpu.VMEM((MG * panel, MG * panel), BF),
            pltpu.VMEM((MG * reaches, MG * panel), BF),
            pltpu.VMEM((classes, MG * panel, LANES), BF),
            pltpu.VMEM((classes, 2 * reaches, 128), BF),
            pltpu.VMEM((LANES, classes * LANES), BF),
            pltpu.VMEM((classes * LANES, LANES), BF),
            pltpu.SemaphoreType.DMA((4,)),
            pltpu.SemaphoreType.DMA((5,)),
            pltpu.SemaphoreType.DMA((groups, 2)),
            pltpu.SemaphoreType.DMA((groups, 2)),
            pltpu.SemaphoreType.DMA((groups, 2)),
            pltpu.SemaphoreType.DMA((groups, 2)),
            pltpu.SemaphoreType.DMA((groups,)),
            pltpu.SemaphoreType.DMA((groups,)),
            pltpu.SemaphoreType.DMA((groups,)),
            pltpu.SemaphoreType.DMA((groups,)),
            pltpu.SemaphoreType.DMA((groups,)),
        ],
        compiler_params=pltpu.CompilerParams(
            collective_id=0, has_side_effects=True, vmem_limit_bytes=56 << 20
        ),
        name="route_levels",
    )(*given)
    return flat.reshape(hours, members, reaches).astype(BF)


def solution(mesh):
    return jax.shard_map(
        functools.partial(local, mesh.shape["region"], mesh.shape["order"]),
        mesh=mesh,
        in_specs=(
            P(None, None, ("region", "order")),
            P("region", "order", None),
            P(("region", "order"), None),
            P(("region", "order"), None),
            P(("region", "order"), None),
            P(),
            P(),
            P("region", "order", None),
            P("region", "order", None, None),
        ),
        out_specs=P(None, None, ("region", "order")),
        check_vma=False,
    )
```

```python
import functools

import jax
import jax.numpy as jnp
from jax import lax
from jax.experimental import pallas as pl
from jax.experimental.pallas import tpu as pltpu
from jax.sharding import PartitionSpec as P

MESH = pl.DeviceIdType.MESH
BF = jnp.bfloat16
NX, NZ = 4, 8
F32 = jnp.float32
LANES = 256
AHEAD = 2
SPARE = 14
PICK = 2
LAG = 4
MG = 4


def mm(a, b):
    return jnp.dot(a, b, preferred_element_type=F32)


def mm_nt(a, b):
    return lax.dot_general(a, b, (((1,), (1,)), ((), ())), preferred_element_type=F32)


def iota(shape, dim):
    return lax.broadcasted_iota(jnp.int32, shape, dim)


def onehot(hits):
    return jnp.where(hits, 1.0, 0.0)


def kernel(
    sizes,
    *refs,
):
    given, out32, held = refs[:9], refs[9], refs[10:19]
    route_body(sizes, given, held, out32, *refs[19:])


def route_body(
    sizes,
    given,
    held,
    out32,
    insem,
    turn_buf,
    own,
    near1,
    near2,
    meta,
    send_n,
    send_f,
    recv,
    inbox,
    outbox,
    lat,
    base_out,
    sel,
    w_hi,
    w_lo,
    wo_hi,
    wo_lo,
    perm,
    scat,
    mask_o,
    mask_c,
    toep,
    toep_t,
    msend,
    mrecv,
    s1s,
    s1r,
    s2s,
    s2r,
    nsem,
    fsem,
    rsem,
    cssem,
    crsem,
):
    hours, members, regions, orders, reaches, classes, panel = sizes
    x_ref, send_rows_ref, idx_ref, w_ref, cls_ref, shape_ref, rate_ref, outlets_ref, inc_ref = held
    groups = members // MG
    soon = AHEAD * MG * 32
    parts = (pl.ds(0, soon), pl.ds(soon, groups * MG * 32 - soon))
    loads = [pltpu.make_async_copy(given[0].at[parts[0]], x_ref.at[parts[0]], insem.at[0])] + [
        pltpu.make_async_copy(given[i], held[i], insem.at[i]) for i in range(1, len(held))
    ]
    others = pltpu.make_async_copy(given[0].at[parts[1]], x_ref.at[parts[1]], insem.at[len(held)])
    for load in loads[:2] + [others] + loads[2:]:
        load.start()
    slots = regions * MG * 4
    r = lax.axis_index("region")
    o = lax.axis_index("order")
    x = r // NZ
    z = lax.rem(r, NZ)
    nxt = lax.rem(o + 1, orders)
    prv = lax.rem(o + orders - 1, orders)

    def at(dx, dz):
        return (lax.rem(x + dx + NX, NX) * NZ + lax.rem(z + dz + NZ, NZ), o)

    barrier = pltpu.get_barrier_semaphore()

    def greet(n, c):
        peer = at(n // 5, lax.rem(n, 5) + NZ - 2)
        pl.semaphore_signal(barrier, inc=1, device_id=peer, device_id_type=MESH)
        return c

    lax.fori_loop(0, 2, greet, 0)
    lax.fori_loop(3, NX * 5, greet, 0)
    pl.semaphore_signal(barrier, inc=1, device_id=(r, prv), device_id_type=MESH)

    filler = jnp.zeros((groups, 2, LANES - hours, 128), BF)
    near1[:, :, hours:LANES] = filler
    near2[:, :, hours:LANES] = filler
    turn_buf[...] = jnp.zeros_like(turn_buf)
    loads[0].wait()

    def cast(g, c):
        rows = MG * 32
        start = pl.multiple_of(g * rows, rows)
        own[g, 0:128] = x_ref[pl.ds(start, rows), 0:128].astype(BF)
        turn_buf[:, 0 : hours - 128] = x_ref[pl.ds(start, rows), 128:hours]
        own[g, 128:LANES] = turn_buf[...].T.astype(BF)
        return c

    lax.fori_loop(0, AHEAD, cast, 0)
    loads[1].wait()
    meta[2] = send_rows_ref[...]
    pl.semaphore_wait(barrier, NX * 5)

    def step1(g):
        for way in range(2):
            pltpu.make_async_remote_copy(
                src_ref=own.at[g, pl.ds(0, hours)],
                dst_ref=near1.at[g, way, pl.ds(0, hours)],
                send_sem=s1s.at[g, way],
                recv_sem=s1r.at[g, way],
                device_id=at(0, 1 - 2 * way),
                device_id_type=MESH,
            ).start()

    def step2(g):
        for way in range(2):
            got = near1.at[g, way, pl.ds(0, hours)]
            pltpu.make_async_copy(got, got, s1r.at[g, way]).wait()
            pltpu.make_async_remote_copy(
                src_ref=got,
                dst_ref=near2.at[g, way, pl.ds(0, hours)],
                send_sem=s2s.at[g, way],
                recv_sem=s2r.at[g, way],
                device_id=at(0, 1 - 2 * way),
                device_id_type=MESH,
            ).start()

    step1(0)
    tell = [
        pltpu.make_async_remote_copy(
            src_ref=send_rows_ref,
            dst_ref=meta.at[2 + dz],
            send_sem=msend.at[n],
            recv_sem=mrecv.at[2 + dz],
            device_id=at(0, dz),
            device_id_type=MESH,
        )
        for n, dz in enumerate((1, -1, 2, -2))
    ]
    for copy in tell:
        copy.start()
    for g in range(1, AHEAD):
        step1(g)
    others.wait()
    lax.fori_loop(AHEAD, groups, cast, 0)
    for load in loads[2:]:
        load.wait()

    diag = iota((classes, classes), 0) == iota((classes, classes), 1)
    rate = jnp.sum(
        jnp.where(diag, jnp.broadcast_to(rate_ref[...], (classes, classes)), 0.0),
        axis=1,
        keepdims=True,
    )
    lag = iota((classes, hours), 1).astype(F32)
    unit = rate * shape_ref[...] * jnp.exp(-rate * lag)
    base_out[0:classes, 128:LANES] = jnp.zeros((classes, LANES - 128), F32)
    base_out[0:classes, 0:hours] = unit.astype(BF).astype(F32)
    later = iota((LANES, LANES), 1) >= iota((LANES, LANES), 0)

    def table(k, c):
        row = jnp.broadcast_to(base_out[pl.ds(k, 1), :], (LANES, LANES))
        turned = pltpu.roll(row, 0, 1, stride=1, stride_axis=0)
        turned = jnp.where(later, turned, 0.0)
        at = pl.multiple_of(k * LANES, LANES)
        toep_t[pl.ds(at, LANES), :] = turned.astype(BF)
        flipped = turned.T.astype(BF)
        here = pl.multiple_of(k * 128, 128)
        toep[:, pl.ds(here, 128)] = flipped[:, 0:128]
        toep[:, pl.ds(here + classes * 128, 128)] = flipped[:, 128:LANES]
        return c

    lax.fori_loop(0, classes, table, 0)

    n0 = iota((slots, 128), 0)
    source = (n0 >> 7) * NZ + ((z + 2 + NZ - ((n0 >> 4) & 7)) & 7)
    pos = source * 4 + (n0 & 3)
    weights_t = jnp.zeros((slots, 128), F32)
    for j in range(4):
        weights_t = weights_t + jnp.where(idx_ref[j : j + 1, :] == pos, w_ref[j : j + 1, :], 0.0)
    weights = weights_t.T
    high = weights.astype(BF)
    low = (weights - high.astype(F32)).astype(BF)
    member_of = (iota((reaches, slots), 1) >> 2) & 3
    for m in range(MG):
        here = onehot(member_of == m).astype(BF)
        w_hi[m * 128 : (m + 1) * 128, :] = high * here
        w_lo[m * 128 : (m + 1) * 128, :] = low * here

    i0 = iota((128, 128), 0)
    i1 = iota((128, 128), 1)
    copies = onehot((iota((128, panel), 0) & 31) == iota((128, panel), 1)).astype(BF)
    at_outlet = onehot(outlets_ref[...] == iota((reaches, panel), 0)).astype(BF)
    outlet_of = mm_nt(copies, at_outlet)
    link_of = mm(copies, inc_ref[...].astype(F32).astype(BF))
    link_t = link_of.T
    for m in range(MG):
        scat[m * 128 : (m + 1) * 128, :] = jnp.where((i1 >> 5) == m, link_t, 0.0).astype(BF)
    outlet_bf = outlet_of.astype(BF)
    mine = ((iota((MG * panel, slots), 1) >> 2) & 3) == (iota((MG * panel, slots), 0) >> 5)
    wo_hi[...] = jnp.where(mine, mm(outlet_bf, high), 0.0).astype(BF)
    wo_lo[...] = jnp.where(mine, mm(outlet_bf, low), 0.0).astype(BF)
    joined = mm_nt(outlet_bf, link_of.astype(BF))
    perm[...] = jnp.where((i0 >> 5) == (i1 >> 5), joined, 0.0).astype(BF)
    cls_c = jnp.broadcast_to(cls_ref[...].astype(F32), (128, 128)).T
    cls_o = mm(outlet_bf, cls_c.astype(BF))
    for k in range(classes):
        hit_c = onehot(cls_c == float(k)).astype(BF)
        hit_o = onehot(cls_o == float(k)).astype(BF)
        for a in range(2):
            mask_o[k, :, a * 128 : (a + 1) * 128] = hit_o
            mask_c[k, a * 128 : (a + 1) * 128, :] = hit_c

    for copy in tell:
        copy.wait_recv()
    k0 = iota((160, 128), 0)
    k1 = iota((160, 128), 1)
    part = k0 >> 6
    for e in range(5):
        way = 1 if e < 2 else 0
        ahead = part * (1 - 2 * way)
        to_x = jnp.where(part == 2, (x + 2 * way + ((k0 >> 4) & 3)) & 3, (k0 >> 4) & 3)
        to_z = (z + ahead + NZ) & 7
        spread = onehot(k1 == (to_x * NZ + to_z) * 4 + (k0 & 3)).astype(BF)
        row_hit = onehot(meta[e] == (iota((128, 128), 0) & 31)).astype(BF)
        picked = mm_nt(spread, row_hit)
        sel[e] = jnp.where(((k0 >> 2) & 3) == (k1 >> 5), picked, 0.0).astype(BF)

    def select(g):
        for way in range(2):
            got = near2.at[g, way, pl.ds(0, hours)]
            pltpu.make_async_copy(got, got, s2r.at[g, way]).wait()
        held_blocks = (near2[g, 1], near1[g, 1], own[g], near1[g, 0], near2[g, 0])
        for e in (0, 4, 1, 2, 3):
            outer = e == 0 or e == 4
            pick = sel[e] if outer else sel[e, 0:64, :]
            block = held_blocks[e]
            taken = jnp.concatenate(
                [mm(pick, block[0:128]), mm_nt(pick, block[128:LANES])], axis=1
            ).astype(BF)
            send_n[g, :, e] = taken[0:64].reshape(NX, MG * 4, LANES)
            if outer:
                way = 0 if e == 4 else 1
                send_f[g, way] = taken[64:160].reshape(6, MG * 4, LANES)

                def far(n, c, way=way):
                    two = n // 4
                    dx = n + two * (2 * way)
                    dz = (1 + two) * (1 - 2 * way)
                    to_x = jnp.where(two == 1, lax.rem(x + dx, NX), n)
                    peer = (to_x * NZ + lax.rem(z + dz + NZ, NZ), o)
                    into = jnp.where(two == 1, 6, 5 + 2 * way)
                    pltpu.make_async_remote_copy(
                        src_ref=send_f.at[g, way, n],
                        dst_ref=recv.at[g, x, into],
                        send_sem=fsem.at[g],
                        recv_sem=rsem.at[g],
                        device_id=peer,
                        device_id_type=MESH,
                    ).start()
                    return c

                lax.fori_loop(0, 6, far, 0)

        def near(d, c):
            to_x = lax.rem(x + d, NX)
            pltpu.make_async_remote_copy(
                src_ref=send_n.at[g, to_x],
                dst_ref=recv.at[g, x, pl.ds(0, 5)],
                send_sem=nsem.at[g],
                recv_sem=rsem.at[g],
                device_id=(to_x * NZ + z, o),
                device_id_type=MESH,
            ).start()
            return c

        lax.fori_loop(1, NX, near, 0)
        pltpu.make_async_copy(send_n.at[g, x], recv.at[g, x, pl.ds(0, 5)], rsem.at[g]).start()

    def route(rows):
        wide = jnp.concatenate([rows * mask_o[k] for k in range(classes)], axis=1)
        return mm(wide, toep_t[...])

    def intake(g):
        pltpu.make_async_copy(recv.at[g], recv.at[g], rsem.at[g]).wait()
        got = recv[g].reshape(slots, LANES)

        @pl.when(o < orders - 1)
        def _():
            base_out[...] = route((mm(wo_hi[...], got) + mm(wo_lo[...], got)).astype(BF))

        @pl.when(o == 0)
        def _():
            outbox[g] = base_out[...].astype(BF)
            pass_on(g)

        lat[g] = mm(w_hi[...], got) + mm(w_lo[...], got)

    def pass_on(g):
        pltpu.make_async_remote_copy(
            src_ref=outbox.at[g],
            dst_ref=inbox.at[g],
            send_sem=cssem.at[g],
            recv_sem=crsem.at[g],
            device_id=(r, nxt),
            device_id_type=MESH,
        ).start()

    def level(g):
        @pl.when(o > 0)
        def _():
            pltpu.make_async_copy(inbox.at[g], inbox.at[g], crsem.at[g]).wait()

        @pl.when(jnp.logical_and(o > 0, o < orders - 1))
        def _():
            moved = mm(perm[...], inbox[g]).astype(BF)
            outbox[g] = (base_out[...] + route(moved)).astype(BF)
            pass_on(g)

    def total(g):
        @pl.when(o > 0)
        def _():
            lat[g] = lat[g] + mm(scat[...], inbox[g])

        def pair(h, c):
            entering = lat[g, pl.ds(pl.multiple_of(h * 256, 256), 256), :].astype(BF)
            early, late_in = [
                jnp.concatenate([entering[:, h : h + 128] * mask_c[k] for k in range(classes)], axis=1)
                for h in (0, 128)
            ]
            flow = mm_nt(toep[0:hours, 0 : classes * 128], early)
            tail = mm_nt(toep[128:hours, classes * 128 :], late_in)
            for m in range(2):
                first = g * MG + h * 2 + m
                cols = slice(m * 128, (m + 1) * 128)
                out32[pl.ds(first, 128, stride=members), :] = flow[0:128, cols]
                out32[pl.ds(first + 128 * members, hours - 128, stride=members), :] = (
                    flow[128:hours, cols] + tail[0 : hours - 128, cols]
                )
            return c

        lax.fori_loop(0, 2, pair, 0)

    late = jnp.minimum(groups, (orders - 1 - o) * SPARE // (orders - 1))

    lag = LAG + o // 3

    def turn(i, c):
        @pl.when(i < groups - AHEAD)
        def _():
            step1(i + AHEAD)

        @pl.when(i < groups)
        def _():
            step2(i)

        @pl.when(jnp.logical_and(i >= PICK, i < groups + PICK))
        def _():
            select(i - PICK)

        @pl.when(jnp.logical_and(i >= lag, i < groups + lag))
        def _():
            intake(i - lag)
            level(i - lag)

            @pl.when(i - lag < groups - late)
            def _():
                total(i - lag)

        return c

    lax.fori_loop(0, groups + LAG + 2, turn, 0)

    def rest(g, c):
        total(g)
        return c

    lax.fori_loop(groups - late, groups, rest, 0)

    for copy in tell:
        copy.wait_send()

    def drain(g, c):
        for way in range(2):
            mine, passed = own.at[g, pl.ds(0, hours)], near1.at[g, way, pl.ds(0, hours)]
            pltpu.make_async_copy(mine, mine, s1s.at[g, way]).wait()
            pltpu.make_async_copy(passed, passed, s2s.at[g, way]).wait()
        sent = send_n.at[g, pl.ds(0, NX - 1)]
        pltpu.make_async_copy(sent, sent, nsem.at[g]).wait()
        pltpu.make_async_copy(send_f.at[g], send_f.at[g], fsem.at[g]).wait()

        @pl.when(o < orders - 1)
        def _():
            pltpu.make_async_copy(outbox.at[g], outbox.at[g], cssem.at[g]).wait()

        return c

    lax.fori_loop(0, groups, drain, 0)


def local(
    regions,
    orders,
    runoff,
    send_rows,
    remap_index,
    remap_weight,
    class_id,
    kernel_shape,
    kernel_rate,
    outlets,
    incidence,
):
    hours, members, rows = runoff.shape
    reaches = remap_index.shape[0]
    classes = kernel_shape.shape[0]
    panel = outlets.shape[2]
    groups = members // MG
    slots = regions * MG * 4
    sizes = (hours, members, regions, orders, reaches, classes, panel)
    given = (
        jnp.transpose(runoff, (1, 2, 0)).reshape(members * rows, hours),
        send_rows.reshape(1, -1),
        remap_index.T,
        remap_weight.T,
        class_id.reshape(1, -1),
        kernel_shape,
        kernel_rate.reshape(1, -1),
        outlets.reshape(1, -1),
        incidence.reshape(panel, reaches),
    )
    flat = pl.pallas_call(
        functools.partial(kernel, sizes),
        out_shape=pltpu.VMEM((hours * members, reaches), F32),
        in_specs=[pl.BlockSpec(memory_space=pltpu.HBM)] * len(given),
        out_specs=pl.BlockSpec(memory_space=pltpu.VMEM),
        scratch_shapes=[pltpu.VMEM(a.shape, a.dtype) for a in given]
        + [
            pltpu.SemaphoreType.DMA((len(given) + 1,)),
            pltpu.VMEM((MG * rows, 128), F32),
            pltpu.VMEM((groups, LANES, MG * rows), BF),
            pltpu.VMEM((groups, 2, LANES, MG * rows), BF),
            pltpu.VMEM((groups, 2, LANES, MG * rows), BF),
            pltpu.VMEM((5, 1, 128), jnp.int32),
            pltpu.VMEM((groups, NX, 5, MG * 4, LANES), BF),
            pltpu.VMEM((groups, 2, 6, MG * 4, LANES), BF),
            pltpu.VMEM((groups, NX, NZ, MG * 4, LANES), BF),
            pltpu.VMEM((groups, MG * panel, LANES), BF),
            pltpu.VMEM((groups, MG * panel, LANES), BF),
            pltpu.VMEM((groups, MG * reaches, LANES), F32),
            pltpu.VMEM((MG * panel, LANES), F32),
            pltpu.VMEM((5, 160, MG * rows), BF),
            pltpu.VMEM((MG * reaches, slots), BF),
            pltpu.VMEM((MG * reaches, slots), BF),
            pltpu.VMEM((MG * panel, slots), BF),
            pltpu.VMEM((MG * panel, slots), BF),
            pltpu.VMEM((MG * panel, MG * panel), BF),
            pltpu.VMEM((MG * reaches, MG * panel), BF),
            pltpu.VMEM((classes, MG * panel, LANES), BF),
            pltpu.VMEM((classes, 2 * reaches, 128), BF),
            pltpu.VMEM((LANES, classes * LANES), BF),
            pltpu.VMEM((classes * LANES, LANES), BF),
            pltpu.SemaphoreType.DMA((4,)),
            pltpu.SemaphoreType.DMA((5,)),
            pltpu.SemaphoreType.DMA((groups, 2)),
            pltpu.SemaphoreType.DMA((groups, 2)),
            pltpu.SemaphoreType.DMA((groups, 2)),
            pltpu.SemaphoreType.DMA((groups, 2)),
            pltpu.SemaphoreType.DMA((groups,)),
            pltpu.SemaphoreType.DMA((groups,)),
            pltpu.SemaphoreType.DMA((groups,)),
            pltpu.SemaphoreType.DMA((groups,)),
            pltpu.SemaphoreType.DMA((groups,)),
        ],
        compiler_params=pltpu.CompilerParams(
            collective_id=0, has_side_effects=True, vmem_limit_bytes=56 << 20
        ),
        name="route_levels",
    )(*given)
    return flat.reshape(hours, members, reaches).astype(BF)


def solution(mesh):
    return jax.shard_map(
        functools.partial(local, mesh.shape["region"], mesh.shape["order"]),
        mesh=mesh,
        in_specs=(
            P(None, None, ("region", "order")),
            P("region", "order", None),
            P(("region", "order"), None),
            P(("region", "order"), None),
            P(("region", "order"), None),
            P(),
            P(),
            P("region", "order", None),
            P("region", "order", None, None),
        ),
        out_specs=P(None, None, ("region", "order")),
        check_vma=False,
    )
```
